32 devices in a mesh: img: 8 (over z, core), pix: 4 (over y, x).
Axes of the slice: x: 2, y: 2, z: 4, core: 2. Of those that a mesh axis runs over, the one named last changes fastest.
Arguments:
- images: bfloat16 [25600, 16384], P('img', 'pix'), may hold values from -6 to 6
- classes: int32 [25600], P('img'), may hold values from 0 to 63
- ctf_table: bfloat16 [64, 16384], P(None, 'pix'), may hold values from -1 to 1, as said below
- weights: float32 [25600], P('img'), may hold values from 0.1 to 1
- probes: float32 [16384, 256], P('pix'), may hold values from -6 to 6
Outputs:
- basis: float32 [16384, 256], P('pix')
- factor: float32 [256, 256], replicated
The draws below stay inside these ranges and needn't reach their ends.
Inputs may be any that keep to these rules, and one draw needn't show every extreme that they name: `ctf_table`: a smooth envelope over the pixel index times an independent magnitude and sign for each entry.
All inputs are finite; a program needn't handle non-finite values.
Results may differ from the reference program's by a relative error of at most 0.012.
Values may be sent and summed in bfloat16 or wider, within the bound.
No kernel may reach another device: no remote copies, remote signals or barrier semaphores. Data moves between devices by JAX's collectives and lax.ppermute only.
A program may use at most 128 MiB of HBM per device.

```python
import math
import jax
import jax.numpy as jnp
from jax import lax

PIXELS = 16384
R = 256
CLASSES = 64
ITERS = 2
IMAGES = 25600


def draw_ctf_table(key, part):
    first_key = jax.random.fold_in(key, 11)
    second_key = jax.random.fold_in(key, 12)
    position = jnp.arange(PIXELS).astype(jnp.float32) / PIXELS
    envelope = jnp.exp(-1.5 * position)
    magnitude = jax.random.uniform(first_key, (CLASSES, PIXELS), jnp.float32, 0.3, 1.0)
    signs = jnp.where(jax.random.bernoulli(second_key, 0.5, (CLASSES, PIXELS)), 1.0, -1.0)
    return (envelope[None, :] * magnitude * signs).astype(jnp.bfloat16)


def plant(array, key, low, high):
    place = [jax.random.randint(jax.random.fold_in(key, axis), (), 0, length) for axis, length in enumerate(array.shape)]
    widest = array.shape.index(max(array.shape))
    next_to = place[:widest] + [(place[widest] + 1) % array.shape[widest]] + place[widest + 1:]
    return array.at[tuple(place)].set(low).at[tuple(next_to)].set(high)


def level_of(rng, extent, shards, least, top_value):
    gain, own = 1.0, jax.random.fold_in(rng, 6)
    for axis_at, shards_of in shards:
        draws = jnp.exp(jax.random.uniform(jax.random.fold_in(own, axis_at), (shards_of,), jnp.float32, least / len(shards), top_value / len(shards)))
        gain = gain * jnp.repeat(draws, extent[axis_at] // shards_of).reshape([-1 if axis == axis_at else 1 for axis in range(len(extent))])
    return gain


def normal_values(stream_key, extent, scale, most, split=(), dtype=jnp.bfloat16):
    array = jax.random.normal(stream_key, extent, jnp.float32) * scale
    if len(split) > 0:
        array = level_of(stream_key, extent, split, -0.22, 0.18) * array
    return jnp.clip(array, min=-most, max=most).astype(dtype)


def setup_inputs(seed: int = 0) -> dict:
    arg_keys = jax.random.split(jax.random.key(seed), 6)
    images = normal_values(arg_keys[0], (IMAGES, PIXELS), 1.0, 6.0, ((0, 8), (1, 4)))
    classes = plant(jax.random.randint(arg_keys[1], (IMAGES,), 0, CLASSES), jax.random.fold_in(arg_keys[1], 1), 0, CLASSES - 1).astype(jnp.int32)
    ctf_table = draw_ctf_table(jax.random.fold_in(arg_keys[5], 71), 0)
    weights = jnp.clip(jnp.exp(math.log(1.0) - 2.3025851 * jax.random.uniform(arg_keys[3], (IMAGES,), jnp.float32) ** level_of(arg_keys[3], (IMAGES,), ((0, 8),), -0.2, 0.2)), 0.1, 1.0)
    probes = normal_values(arg_keys[4], (PIXELS, R), 1.0, 6.0, ((0, 4),), jnp.float32)
    return {"images": images, "classes": classes, "ctf_table": ctf_table, "weights": weights, "probes": probes}


def reference(images, classes, ctf_table, weights, probes):
    filters = ctf_table[classes].astype(jnp.float32)
    filtered = (images.astype(jnp.float32) * filters).astype(jnp.bfloat16)
    current = probes
    factor = jnp.zeros((R, R), jnp.float32)
    for sweep in range(ITERS):
        probe_half = current.astype(jnp.bfloat16)
        scores = jnp.dot(filtered.astype(jnp.float32), probe_half.astype(jnp.float32), preferred_element_type=jnp.float32)
        scaled = (weights[:, None] * scores).astype(jnp.bfloat16)
        image_sum = jnp.dot(filtered.T.astype(jnp.float32), scaled.astype(jnp.float32), preferred_element_type=jnp.float32)
        gram_matrix = jnp.dot(image_sum.T, image_sum, precision=lax.Precision.HIGHEST)
        factor = jnp.linalg.cholesky(gram_matrix)
        current = jax.scipy.linalg.solve_triangular(factor, image_sum.T, lower=True).T
    return (current, factor)
```

```python
import functools

import jax
import jax.numpy as jnp
from jax import lax
from jax.experimental import pallas as pl
from jax.experimental.pallas import tpu as pltpu
from jax.sharding import PartitionSpec as P

ITERS = 2
F32 = jnp.float32
BF16 = jnp.bfloat16
LANES = 128
PANEL = 32
HIGHEST = lax.Precision.HIGHEST


def cost(flops, nbytes):
    return pl.CostEstimate(flops=int(flops), bytes_accessed=int(nbytes), transcendentals=0)


def vmem(nbytes):
    return pltpu.CompilerParams(vmem_limit_bytes=nbytes)


def row_tile(rows, most=400):
    return max(t for t in range(16, most + 1, 16) if rows % t == 0)


def xor_swap(value, axis, mask):
    size = lax.axis_size(axis)
    return lax.ppermute(value, axis, [(i, i ^ mask) for i in range(size)])


def contract_rows(left, right):
    return lax.dot_general(left, right, (((0,), (0,)), ((), ())), preferred_element_type=F32)


def filter_kernel(order, class_ref, image_ref, table_ref, probe_ref, filtered_ref, score_ref):
    table_rows = table_ref.shape[0]
    rows, pixels = image_ref.shape
    onehot = (
        lax.broadcasted_iota(jnp.int32, (table_rows, rows), 0) == class_ref[0]
    ).astype(BF16)
    filters = contract_rows(onehot, table_ref[...])
    filtered = (image_ref[...].astype(F32) * filters).astype(BF16)
    filtered_ref[...] = filtered
    scores = jnp.dot(filtered, probe_ref[...], preferred_element_type=F32)
    score_ref[...] = scores.astype(score_ref.dtype)


def filter_and_score(order, images, classes, table, probe_half, chunk, out_type):
    rows, pixels = images.shape
    columns = probe_half.shape[1]
    tile = row_tile(chunk)
    steps = chunk // tile
    return pl.pallas_call(
        filter_kernel,
        grid_spec=pltpu.PrefetchScalarGridSpec(
            num_scalar_prefetch=1,
            grid=(steps,),
            in_specs=[
                pl.BlockSpec((1, 1, tile), lambda i, order: (order[0] * steps + i, 0, 0)),
                pl.BlockSpec((tile, pixels), lambda i, order: (order[0] * steps + i, 0)),
                pl.BlockSpec(table.shape, lambda i, order: (0, 0)),
                pl.BlockSpec(probe_half.shape, lambda i, order: (0, 0)),
            ],
            out_specs=[
                pl.BlockSpec((tile, pixels), lambda i, order: (i, 0)),
                pl.BlockSpec((tile, columns), lambda i, order: (i, 0)),
            ],
        ),
        out_shape=[
            jax.ShapeDtypeStruct((chunk, pixels), BF16),
            jax.ShapeDtypeStruct((chunk, columns), out_type),
        ],
        compiler_params=vmem(56 * 2**20),
        cost_estimate=cost(4 * chunk * pixels * columns, 4 * chunk * pixels),
        name="filter_and_score",
    )(order, classes.reshape(rows // tile, 1, tile), images, table, probe_half)


def score_kernel(order, filtered_ref, *refs):
    *basis_refs, score_ref = refs
    width = basis_refs[0].shape[0]
    total = None
    for at, basis_ref in enumerate(basis_refs):
        columns = pl.ds(pl.multiple_of(order[at] * width, width), width)
        term = jnp.dot(filtered_ref[:, columns], basis_ref[...], preferred_element_type=F32)
        total = term if total is None else total + term
    score_ref[...] = total.astype(score_ref.dtype)


def score(order, filtered, basis, out_type):
    rows, pixels = filtered.shape
    columns = basis[0].shape[1]
    tile = row_tile(rows)
    return pl.pallas_call(
        score_kernel,
        grid_spec=pltpu.PrefetchScalarGridSpec(
            num_scalar_prefetch=1,
            grid=(rows // tile,),
            in_specs=[pl.BlockSpec((tile, pixels), lambda i, order: (i, 0))]
            + [pl.BlockSpec(b.shape, lambda i, order: (0, 0)) for b in basis],
            out_specs=pl.BlockSpec((tile, columns), lambda i, order: (i, 0)),
        ),
        out_shape=jax.ShapeDtypeStruct((rows, columns), out_type),
        compiler_params=vmem(40 * 2**20),
        cost_estimate=cost(2 * rows * pixels * columns, 2 * rows * pixels),
        name="score",
    )(order, filtered, *basis)


def sum_blocks(filtered_refs, scaled_refs):
    rows = filtered_refs[0].shape[0]
    whole = rows // 256 * 256
    total = None
    for filtered_ref, scaled_ref in zip(filtered_refs, scaled_refs):
        if whole:
            term = contract_rows(filtered_ref[:whole, :], scaled_ref[:whole, :])
            total = term if total is None else total + term
    if whole < rows:
        left = jnp.concatenate([ref[whole:, :] for ref in filtered_refs], 0)
        right = jnp.concatenate([ref[whole:, :] for ref in scaled_refs], 0)
        term = contract_rows(left, right)
        total = term if total is None else total + term
    return total


def first_sum_kernel(count, order, *refs):
    refs[-1][...] = sum_blocks(refs[:count], refs[count : 2 * count])


def last_sum_kernel(count, half, order, *refs):
    *refs, send_ref, keep_ref = refs
    total = sum_blocks(refs[:count], refs[count : 2 * count]) + refs[-1][...]
    at = pl.program_id(0)

    @pl.when(at < half)
    def _():
        send_ref[...] = total.astype(BF16)

    @pl.when(at >= half)
    def _():
        keep_ref[...] = total.astype(BF16)


def image_sum_specs(filtered, scaled, width):
    rows = filtered[0].shape[0]
    return [pl.BlockSpec((rows, width), lambda i, order: (0, order[i])) for _ in filtered] + [
        pl.BlockSpec(s.shape, lambda i, order: (0, 0)) for s in scaled
    ]


def first_sum(order, filtered, scaled):
    blocks = order.shape[0]
    rows, pixels = filtered[0].shape
    columns = scaled[0].shape[1]
    width = pixels // blocks
    return pl.pallas_call(
        functools.partial(first_sum_kernel, len(filtered)),
        grid_spec=pltpu.PrefetchScalarGridSpec(
            num_scalar_prefetch=1,
            grid=(blocks,),
            in_specs=image_sum_specs(filtered, scaled, width),
            out_specs=pl.BlockSpec((width, columns), lambda i, order: (i, 0)),
        ),
        out_shape=jax.ShapeDtypeStruct((pixels, columns), F32),
        compiler_params=vmem(40 * 2**20),
        cost_estimate=cost(
            2 * len(filtered) * rows * pixels * columns,
            2 * len(filtered) * rows * pixels + 4 * pixels * columns,
        ),
        name="first_sum",
    )(order, *filtered, *scaled)


def last_sum(order, filtered, scaled, partial):
    blocks = order.shape[0]
    half = blocks // 2
    rows, pixels = filtered[0].shape
    columns = scaled[0].shape[1]
    width = pixels // blocks
    return pl.pallas_call(
        functools.partial(last_sum_kernel, len(filtered), half),
        grid_spec=pltpu.PrefetchScalarGridSpec(
            num_scalar_prefetch=1,
            grid=(blocks,),
            in_specs=image_sum_specs(filtered, scaled, width)
            + [pl.BlockSpec((width, columns), lambda i, order: (i, 0))],
            out_specs=[
                pl.BlockSpec((width, columns), lambda i, order: (jnp.minimum(i, half - 1), 0)),
                pl.BlockSpec((width, columns), lambda i, order: (jnp.maximum(i - half, 0), 0)),
            ],
        ),
        out_shape=[jax.ShapeDtypeStruct((pixels // 2, columns), BF16)] * 2,
        compiler_params=vmem(40 * 2**20),
        cost_estimate=cost(
            2 * len(filtered) * rows * pixels * columns,
            2 * len(filtered) * rows * pixels + 6 * pixels * columns,
        ),
        name="last_sum",
    )(order, *filtered, *scaled, partial)


def tree_sum(terms):
    while len(terms) > 1:
        terms = [terms[i] + terms[i + 1] for i in range(0, len(terms), 2)]
    return terms[0]


def gram_kernel(*refs):
    *basis_refs, gram_ref = refs
    gram_ref[...] = tree_sum([contract_rows(ref[...], ref[...]) for ref in basis_refs])


def gram_of(basis):
    rows, columns = basis[0].shape
    return pl.pallas_call(
        gram_kernel,
        out_shape=jax.ShapeDtypeStruct((columns, columns), F32),
        compiler_params=vmem(24 * 2**20),
        cost_estimate=cost(2 * len(basis) * rows * columns * columns, 2 * len(basis) * rows * columns),
        name="gram",
    )(*basis)


def cholesky_kernel(gram_ref, factor_ref, inverse_ref, work_ref):
    size = gram_ref.shape[0]
    work_ref[:, :size] = gram_ref[...]
    square = (size, size)
    row_at = lax.broadcasted_iota(jnp.int32, square, 0)
    column_at = lax.broadcasted_iota(jnp.int32, square, 1)
    work_ref[:, size:] = (row_at == column_at).astype(F32)
    panel_row = lax.broadcasted_iota(jnp.int32, (PANEL, LANES), 0)
    panel_column = lax.broadcasted_iota(jnp.int32, (PANEL, LANES), 1)
    per_tile = LANES // PANEL

    def panel(block, carry):
        start = pl.multiple_of(block * PANEL, PANEL)
        tile = pl.multiple_of((block // per_tile) * LANES, LANES)
        body = work_ref[pl.ds(start, PANEL), :]
        diagonal = work_ref[pl.ds(start, PANEL), pl.ds(tile, LANES)]
        diagonal = pltpu.roll(diagonal, (LANES - (block % per_tile) * PANEL) % LANES, 1)
        for at in range(PANEL):
            column = jnp.broadcast_to(diagonal[:, at : at + 1], (PANEL, LANES))
            scale = jnp.where(panel_row > at, column * (1.0 / column[at : at + 1, :]), 0.0)
            wide = jnp.concatenate([scale] * (body.shape[1] // LANES), 1)
            body = body - wide * body[at : at + 1, :]
            diagonal = diagonal - scale * diagonal[at : at + 1, :]
        pivots = jnp.sum(
            jnp.where(panel_row == panel_column, diagonal, 0.0), axis=1, keepdims=True
        )
        body = body * lax.rsqrt(pivots)
        work_ref[pl.ds(start, PANEL), :] = body
        left = body[:, :size]
        later = lax.broadcasted_iota(jnp.int32, left.shape, 1) >= start + PANEL
        work_ref[...] -= lax.dot_general(
            jnp.where(later, left, 0.0),
            body,
            (((0,), (0,)), ((), ())),
            precision=HIGHEST,
            preferred_element_type=F32,
        )
        return carry

    lax.fori_loop(0, size // PANEL, panel, 0)
    factor_ref[...] = jnp.where(row_at <= column_at, work_ref[:, :size], 0.0).T
    inverse_ref[...] = work_ref[:, size:]


def cholesky_and_inverse(gram):
    size = gram.shape[0]
    return pl.pallas_call(
        cholesky_kernel,
        out_shape=[jax.ShapeDtypeStruct((size, size), F32)] * 2,
        scratch_shapes=[pltpu.VMEM((size, 2 * size), F32)],
        compiler_params=vmem(16 * 2**20),
        cost_estimate=cost(12e9, 12 * size * size),
        name="cholesky",
    )(gram)


def apply_kernel(order, inverse_ref, *refs):
    *basis_refs, out_ref = refs
    inverse = inverse_ref[...]
    parts = []
    for _ in range(3):
        parts.append(inverse.astype(BF16))
        inverse = inverse - parts[-1].astype(F32)
    for at, basis_ref in enumerate(basis_refs):

        @pl.when(pl.program_id(0) == at)
        def _():
            block = basis_ref[...]
            out_ref[...] = sum(
                lax.dot_general(
                    block, part, (((1,), (1,)), ((), ())), preferred_element_type=F32
                )
                for part in reversed(parts)
            )


def apply_inverse(order, inverse, basis):
    rows, columns = basis[0].shape
    blocks = len(basis)
    return pl.pallas_call(
        apply_kernel,
        grid_spec=pltpu.PrefetchScalarGridSpec(
            num_scalar_prefetch=1,
            grid=(blocks,),
            in_specs=[pl.BlockSpec(inverse.shape, lambda i, order: (0, 0))]
            + [pl.BlockSpec((rows, columns), lambda i, order: (0, 0)) for _ in basis],
            out_specs=pl.BlockSpec((rows, columns), lambda i, order: (order[i], 0)),
        ),
        out_shape=jax.ShapeDtypeStruct((rows * blocks, columns), F32),
        compiler_params=vmem(32 * 2**20),
        cost_estimate=cost(6 * rows * blocks * columns * columns, 6 * rows * blocks * columns),
        name="apply",
    )(order, inverse, *basis)


def per_device(images, classes, ctf_table, weights, probes):
    images_here, pixels = images.shape
    pix, img = lax.axis_size("pix"), lax.axis_size("img")
    depth = img // 2
    chunk = images_here // pix
    me = lax.axis_index("pix")
    place = lax.axis_index("img")
    core, level = place % 2, place // 2

    at = jnp.arange(img)
    gathered = ((at // depth) ^ core) * depth + ((at % depth) ^ level)
    scattered = ((1 - at // depth) ^ core) * depth + ((at % depth) ^ level)
    gathered, scattered = gathered.astype(jnp.int32), scattered.astype(jnp.int32)

    shifts = list(range(pix - 1, -1, -1))
    weight_share = lax.dynamic_slice_in_dim(weights, me * chunk, chunk, 0)[:, None]

    filtered, own, arrived = [None] * pix, None, []
    probe_half = probes.astype(BF16)
    for shift in shifts:
        order = (me ^ shift).astype(jnp.int32)[None]
        filtered[shift], part = filter_and_score(
            order, images, classes, ctf_table, probe_half, chunk, BF16 if shift else F32
        )
        if shift:
            arrived.append(xor_swap(part, "pix", shift))
        else:
            own = part

    inverse = None
    for sweep in range(ITERS):
        shares = own
        for part in arrived:
            shares = shares + part.astype(F32)
        if inverse is not None:
            shares = lax.dot_general(
                shares, inverse, (((1,), (1,)), ((), ())), precision=HIGHEST
            )
        scaled_share = (weight_share * shares).astype(BF16)
        scaled = [scaled_share] + [xor_swap(scaled_share, "pix", s) for s in range(1, pix)]
        split = pix // 2
        partial = first_sum(scattered, filtered[:split], scaled[:split])
        send, keep = last_sum(scattered, filtered[split:], scaled[split:], partial)

        got = xor_swap(send, "img", 1)
        width = pixels // img
        pairs = [
            keep[s * width : (s + 1) * width].astype(F32)
            + got[s * width : (s + 1) * width].astype(F32)
            for s in range(depth)
        ]
        total = pairs[0]
        for s in range(depth - 1, 0, -1):
            total = total + xor_swap(pairs[s].astype(BF16), "img", 2 * s).astype(F32)
        half = total.astype(BF16)
        near = [half] + [xor_swap(half, "img", 2 * s) for s in range(1, depth)]
        basis = near + [xor_swap(block, "img", 1) for block in near]

        gram = gram_of(basis)
        step = 1
        while step < pix:
            gram = gram + xor_swap(gram, "pix", step)
            step *= 2
        factor, inverse = cholesky_and_inverse(gram)
        if sweep == ITERS - 1:
            return apply_inverse(gathered, inverse, basis), factor
        own, arrived = None, []
        for shift in shifts:
            part = score(gathered, filtered[shift], basis, BF16 if shift else F32)
            if shift:
                arrived.append(xor_swap(part, "pix", shift))
            else:
                own = part


def plain_per_device(images, classes, ctf_table, weights, probes):
    onehot = (classes[:, None] == jnp.arange(ctf_table.shape[0])[None, :]).astype(BF16)
    filters = jnp.dot(onehot, ctf_table, preferred_element_type=F32)
    filtered = (images.astype(F32) * filters).astype(BF16)
    current = probes
    factor = None
    for sweep in range(ITERS):
        share_rows = filtered.shape[0] // lax.axis_size("pix")
        shares = lax.psum_scatter(
            jnp.dot(filtered, current.astype(BF16), preferred_element_type=F32),
            "pix",
            scatter_dimension=0,
            tiled=True,
        )
        weight_share = lax.dynamic_slice_in_dim(
            weights, lax.axis_index("pix") * share_rows, share_rows, 0
        )
        scaled_share = (weight_share[:, None] * shares).astype(BF16)
        scaled = lax.all_gather(scaled_share, "pix", axis=0, tiled=True)
        image_sum = lax.psum(contract_rows(filtered, scaled), "img")
        gram = lax.psum(jnp.dot(image_sum.T, image_sum, precision=HIGHEST), "pix")
        factor = jnp.linalg.cholesky(gram)
        current = jax.scipy.linalg.solve_triangular(factor, image_sum.T, lower=True).T
    return current, factor


def power_of_two(n):
    return n > 1 and n & (n - 1) == 0


def per_device_of(images, classes, ctf_table, weights, probes):
    rows, pixels = images.shape
    pix, img = lax.axis_size("pix"), lax.axis_size("img")
    columns = probes.shape[1]
    fits = (
        power_of_two(pix)
        and power_of_two(img)
        and rows % (16 * pix) == 0
        and pixels % (LANES * img) == 0
        and columns % LANES == 0
    )
    run = per_device if fits else plain_per_device
    return run(images, classes, ctf_table, weights, probes)


def solution(mesh):
    in_specs = (P("img", "pix"), P("img"), P(None, "pix"), P("img"), P("pix", None))
    out_specs = (P("pix", None), P())
    return jax.shard_map(
        per_device_of, mesh=mesh, in_specs=in_specs, out_specs=out_specs, check_vma=False
    )
```

```python
import functools

import jax
import jax.numpy as jnp
from jax import lax
from jax.experimental import pallas as pl
from jax.experimental.pallas import tpu as pltpu
from jax.sharding import PartitionSpec as P

ITERS = 2
F32 = jnp.float32
BF16 = jnp.bfloat16
LANES = 128
PANEL = 32
GROUP = 8
HIGHEST = lax.Precision.HIGHEST


def cost(flops, nbytes):
    return pl.CostEstimate(flops=int(flops), bytes_accessed=int(nbytes), transcendentals=0)


def vmem(nbytes):
    return pltpu.CompilerParams(vmem_limit_bytes=nbytes)


def row_tile(rows, most=400):
    return max(t for t in range(16, most + 1, 16) if rows % t == 0)


def xor_swap(value, axis, mask):
    size = lax.axis_size(axis)
    return lax.ppermute(value, axis, [(i, i ^ mask) for i in range(size)])


def contract_rows(left, right):
    return lax.dot_general(left, right, (((0,), (0,)), ((), ())), preferred_element_type=F32)


def in_vmem():
    return pl.BlockSpec(memory_space=pltpu.VMEM)


def filter_kernel(places, class_ref, image_ref, table_ref, probe_ref, filtered_ref, score_ref):
    table_rows = table_ref.shape[0]
    rows, pixels = image_ref.shape
    onehot = (
        lax.broadcasted_iota(jnp.int32, (table_rows, rows), 0) == class_ref[0]
    ).astype(BF16)
    here = pl.ds(pl.multiple_of(pl.program_id(0) * rows, rows), rows)
    scores = None
    width = min(pixels, 8 * LANES)
    for at in range(0, pixels, width):
        columns = slice(at, min(at + width, pixels))
        filters = contract_rows(onehot, table_ref[:, columns])
        filtered = (image_ref[:, columns].astype(F32) * filters).astype(BF16)
        filtered_ref[here, columns] = filtered
        term = jnp.dot(filtered, probe_ref[columns, :], preferred_element_type=F32)
        scores = term if scores is None else scores + term
    score_ref[here, :] = scores.astype(score_ref.dtype)


def filter_and_score(places, shift, images, classes, table, probe_half, chunk, out_type):
    rows, pixels = images.shape
    columns = probe_half.shape[1]
    tile = row_tile(chunk)
    steps = chunk // tile
    return pl.pallas_call(
        filter_kernel,
        grid_spec=pltpu.PrefetchScalarGridSpec(
            num_scalar_prefetch=1,
            grid=(steps,),
            in_specs=[
                pl.BlockSpec((1, 1, tile), lambda i, places: (places[shift] * steps + i, 0, 0)),
                pl.BlockSpec((tile, pixels), lambda i, places: (places[shift] * steps + i, 0)),
                in_vmem(),
                in_vmem(),
            ],
            out_specs=[in_vmem(), in_vmem()],
        ),
        out_shape=[
            pltpu.VMEM((chunk, pixels), BF16),
            jax.ShapeDtypeStruct((chunk, columns), out_type),
        ],
        compiler_params=vmem(14 * 2**20),
        cost_estimate=cost(4 * chunk * pixels * columns, 2 * chunk * pixels),
        name="filter_and_score",
    )(places, classes.reshape(rows // tile, 1, tile), images, table, probe_half)


def prefetched(count, outs):
    return pltpu.PrefetchScalarGridSpec(
        num_scalar_prefetch=1,
        grid=(),
        in_specs=[in_vmem()] * count,
        out_specs=[in_vmem()] * outs,
    )


def score_kernel(first, places, filtered_ref, *refs):
    *basis_refs, score_ref = refs
    width = basis_refs[0].shape[0]
    total = None
    for at, basis_ref in enumerate(basis_refs):
        columns = pl.ds(pl.multiple_of(places[first + at] * width, width), width)
        term = jnp.dot(filtered_ref[:, columns], basis_ref[...], preferred_element_type=F32)
        total = term if total is None else total + term
    score_ref[...] = total.astype(score_ref.dtype)


def score(places, first, filtered, basis, out_type):
    rows, pixels = filtered.shape
    columns = basis[0].shape[1]
    return pl.pallas_call(
        functools.partial(score_kernel, first),
        grid_spec=prefetched(1 + len(basis), 1),
        out_shape=[jax.ShapeDtypeStruct((rows, columns), out_type)],
        compiler_params=vmem(16 * 2**20),
        cost_estimate=cost(2 * rows * pixels * columns, 2 * rows * columns),
        name="score",
    )(places, filtered, *basis)[0]


def sum_blocks(filtered, scaled):
    rows = filtered[0].shape[0]
    whole = rows // 256 * 256
    total = None
    for left, right in zip(filtered, scaled):
        if whole:
            term = contract_rows(left[:whole, :], right[:whole, :])
            total = term if total is None else total + term
    if whole < rows:
        left = jnp.concatenate([block[whole:, :] for block in filtered], 0)
        right = jnp.concatenate([block[whole:, :] for block in scaled], 0)
        term = contract_rows(left, right)
        total = term if total is None else total + term
    return total


def image_sum_kernel(count, first, places, *refs):
    filtered_refs, scaled_refs = refs[:count], refs[count : 2 * count]
    send_ref, keep_ref = refs[-2:]
    width = send_ref.shape[0]

    def block(at, carry):
        columns = pl.ds(pl.multiple_of(places[first + at] * width, width), width)
        total = sum_blocks(
            [ref[:, columns] for ref in filtered_refs], [ref[...] for ref in scaled_refs]
        )

        @pl.when(at == 0)
        def _():
            send_ref[...] = total.astype(send_ref.dtype)

        @pl.when(at == 1)
        def _():
            keep_ref[...] = total

        return carry

    lax.fori_loop(0, 2, block, 0)


def image_sum(places, first, filtered, scaled, width, after):
    count = len(filtered)
    rows = filtered[0].shape[0]
    columns = scaled[0].shape[1]
    return pl.pallas_call(
        functools.partial(image_sum_kernel, count, first),
        grid_spec=prefetched(2 * count + len(after), 2),
        out_shape=[
            jax.ShapeDtypeStruct((width, columns), BF16),
            jax.ShapeDtypeStruct((width, columns), F32),
        ],
        compiler_params=vmem(16 * 2**20),
        cost_estimate=cost(4 * count * rows * width * columns, 6 * width * columns),
        name="image_sum",
    )(places, *filtered, *scaled, *after)


def tree_sum(terms):
    while len(terms) > 1:
        terms = [terms[i] + terms[i + 1] for i in range(0, len(terms), 2)]
    return terms[0]


def gram_kernel(core_at, places, *refs):
    *basis_refs, _, half_ref, gram_ref = refs
    gram_ref[...] = tree_sum([contract_rows(ref[...], ref[...]) for ref in basis_refs])
    rows = half_ref.shape[0]
    half_ref[...] = gram_ref[pl.ds(pl.multiple_of(places[core_at] * rows, rows), rows), :]


def half_gram(places, core_at, basis, after):
    rows, columns = basis[0].shape
    return pl.pallas_call(
        functools.partial(gram_kernel, core_at),
        grid_spec=pltpu.PrefetchScalarGridSpec(
            num_scalar_prefetch=1,
            grid=(),
            in_specs=[in_vmem()] * (len(basis) + 1),
            out_specs=[in_vmem()],
            scratch_shapes=[pltpu.VMEM((columns, columns), F32)],
        ),
        out_shape=[jax.ShapeDtypeStruct((columns // 2, columns), F32)],
        compiler_params=vmem(12 * 2**20),
        cost_estimate=cost(2 * len(basis) * rows * columns * columns, 2 * len(basis) * rows * columns),
        name="gram",
    )(places, *basis, after)[0]


def normalize_kernel(core_at, scale, places, *refs):
    *part_refs, inverse_ref, half_ref, send_ref, keep_ref, gram_ref = refs
    total = part_refs[0][...]
    for ref in part_refs[1:]:
        total = total + ref[...].astype(F32)
    block = lax.dot_general(
        total,
        inverse_ref[...] * scale,
        (((1,), (1,)), ((), ())),
        precision=HIGHEST,
        preferred_element_type=F32,
    ).astype(BF16)
    half_ref[...] = block
    gram_ref[...] = contract_rows(block, block)
    rows = send_ref.shape[0]
    here = places[core_at]
    send_ref[...] = gram_ref[pl.ds(pl.multiple_of((1 - here) * rows, rows), rows), :]
    keep_ref[...] = gram_ref[pl.ds(pl.multiple_of(here * rows, rows), rows), :]


def normalize_and_gram(places, core_at, parts, inverse, scale):
    rows, columns = parts[0].shape
    return pl.pallas_call(
        functools.partial(normalize_kernel, core_at, scale),
        grid_spec=pltpu.PrefetchScalarGridSpec(
            num_scalar_prefetch=1,
            grid=(),
            in_specs=[in_vmem()] * (len(parts) + 1),
            out_specs=[in_vmem()] * 3,
            scratch_shapes=[pltpu.VMEM((columns, columns), F32)],
        ),
        out_shape=[
            jax.ShapeDtypeStruct((rows, columns), BF16),
            jax.ShapeDtypeStruct((columns // 2, columns), F32),
            jax.ShapeDtypeStruct((columns // 2, columns), F32),
        ],
        compiler_params=vmem(12 * 2**20),
        cost_estimate=cost(14 * rows * columns * columns, 8 * rows * columns),
        name="normalize",
    )(places, *parts, inverse)


def scatter_kernel(first, places, keep_ref, got_ref, *piece_refs):
    rows = piece_refs[0].shape[0]
    for at, ref in enumerate(piece_refs):
        here = pl.ds(pl.multiple_of(places[first + at] * rows, rows), rows)
        ref[...] = keep_ref[here, :] + got_ref[here, :]


def scatter_rows(places, first, keep, got, count):
    rows, columns = keep.shape
    return pl.pallas_call(
        functools.partial(scatter_kernel, first),
        grid_spec=prefetched(2, count),
        out_shape=[jax.ShapeDtypeStruct((rows // count, columns), F32)] * count,
        compiler_params=vmem(4 * 2**20),
        cost_estimate=cost(rows * columns, 12 * rows * columns),
        name="scatter",
    )(places, keep, got)


def gather_kernel(first, count, places, *refs):
    piece_refs, (block_ref, out_ref, block_out_ref) = refs[:count], refs[count:]
    rows = piece_refs[0].shape[0]
    for at, ref in enumerate(piece_refs):
        out_ref[pl.ds(pl.multiple_of(places[first + at] * rows, rows), rows), :] = ref[...]
    block_out_ref[...] = block_ref[...]


def gather_rows(places, first, pieces, block):
    count = len(pieces)
    rows, columns = pieces[0].shape
    return pl.pallas_call(
        functools.partial(gather_kernel, first, count),
        grid_spec=prefetched(count + 1, 2),
        out_shape=[
            jax.ShapeDtypeStruct((rows * count, columns), F32),
            jax.ShapeDtypeStruct(block.shape, block.dtype),
        ],
        compiler_params=vmem(4 * 2**20),
        cost_estimate=cost(rows * columns, 8 * count * rows * columns),
        name="gather",
    )(places, *pieces, block)


def square_places(size):
    return tuple(lax.broadcasted_iota(jnp.int32, (size, size), axis) for axis in (0, 1))


def split_in_three(value):
    parts = []
    for _ in range(3):
        parts.append(value.astype(BF16))
        value = value - parts[-1].astype(F32)
    return parts


def contract_rows_fully(left, right):
    l0, l1, l2 = split_in_three(left)
    r0, r1, r2 = split_in_three(right)
    return contract_rows(
        jnp.concatenate([l2, l1, l0, l1, l0, l0], 0), jnp.concatenate([r0, r1, r2, r0, r1, r0], 0)
    )


def eliminate(work_ref, first, last):
    size = work_ref.shape[0]
    panel_row = lax.broadcasted_iota(jnp.int32, (PANEL, LANES), 0)
    panel_column = lax.broadcasted_iota(jnp.int32, (PANEL, LANES), 1)
    per_tile = LANES // PANEL

    def panel(block, carry):
        start = pl.multiple_of(block * PANEL, PANEL)
        tile = pl.multiple_of((block // per_tile) * LANES, LANES)
        diagonal = work_ref[pl.ds(start, PANEL), pl.ds(tile, LANES)]
        diagonal = pltpu.roll(diagonal, (LANES - (block % per_tile) * PANEL) % LANES, 1)
        tiles = [diagonal] + [
            work_ref[pl.ds(start, PANEL), at : at + LANES] for at in range(0, 2 * size, LANES)
        ]
        for top in range(0, PANEL, GROUP):
            tiles = eliminate_group(tiles, panel_row, top)
        pivots = jnp.sum(jnp.where(panel_row == panel_column, tiles[0], 0.0), axis=1, keepdims=True)
        body = jnp.concatenate(tiles[1:], 1) * lax.rsqrt(pivots)
        work_ref[pl.ds(start, PANEL), :] = body
        left = body[:, :size]
        later = lax.broadcasted_iota(jnp.int32, left.shape, 1) >= start + PANEL
        work_ref[...] -= contract_rows_fully(jnp.where(later, left, 0.0), body)
        return carry

    lax.fori_loop(first, last, panel, 0)


def eliminate_group(tiles, panel_row, top):
    shape = panel_row.shape
    columns = [
        jnp.broadcast_to(tiles[0][:, top + k : top + k + 1], shape) for k in range(GROUP)
    ]
    block = [[columns[k][top + i : top + i + 1, :] for k in range(i + 1)] for i in range(GROUP)]
    ratio = [[None] * GROUP for _ in range(GROUP)]
    scales = []
    for k in range(GROUP):
        inverse = 1.0 / block[k][k]
        for i in range(k + 1, GROUP):
            ratio[i][k] = block[i][k] * inverse
        for i in range(k + 1, GROUP):
            for m in range(k + 1, i + 1):
                block[i][m] = block[i][m] - ratio[i][k] * block[m][k]
        scales.append(jnp.where(panel_row > top + k, columns[k] * inverse, 0.0))
        for m in range(k + 1, GROUP):
            columns[m] = columns[m] - scales[k] * block[m][k]
    result = []
    for tile in tiles:
        rows = [tile[top + k : top + k + 1, :] for k in range(GROUP)]
        for k in range(GROUP):
            for m in range(k + 1, GROUP):
                rows[m] = rows[m] - ratio[m][k] * rows[k]
        for k in range(GROUP):
            tile = tile - scales[k] * rows[k]
        result.append(tile)
    return result


def cholesky_kernel(first, last, place_at, places, *refs):
    size = refs[-1].shape[0]
    panels = size // PANEL
    row_at, column_at = square_places(size)
    if first == 0:
        *piece_refs, = refs[: -1 if last < panels else -3]
        work_ref = refs[-1]
        rows = piece_refs[0].shape[0]
        for at, ref in enumerate(piece_refs):
            here = pl.ds(pl.multiple_of(places[place_at + at] * rows, rows), rows)
            work_ref[here, :size] = ref[...]
        work_ref[:, size:] = (row_at == column_at).astype(F32)
    else:
        work_ref = refs[-1]
        work_ref[...] = refs[0][...]
    eliminate(work_ref, first, last)
    if last == panels:
        factor_ref, inverse_ref = refs[-3:-1]
        factor_ref[...] = jnp.where(row_at <= column_at, work_ref[:, :size], 0.0).T
        inverse_ref[...] = work_ref[:, size:]


def cholesky_and_inverse(places, place_at, pieces, calls):
    size = pieces[0].shape[1]
    panels = size // PANEL
    state = pieces
    for call in range(calls):
        first, last = panels * call // calls, panels * (call + 1) // calls
        work = jax.ShapeDtypeStruct((size, 2 * size), F32)
        square = jax.ShapeDtypeStruct((size, size), F32)
        final = last == panels
        state = pl.pallas_call(
            functools.partial(cholesky_kernel, first, last, place_at),
            grid_spec=pltpu.PrefetchScalarGridSpec(
                num_scalar_prefetch=1,
                grid=(),
                in_specs=[in_vmem()] * len(state),
                out_specs=[in_vmem()] * (2 if final else 1),
                scratch_shapes=[pltpu.VMEM(work.shape, F32)] if final else [],
            ),
            out_shape=[square, square] if final else [work],
            compiler_params=vmem(12 * 2**20),
            cost_estimate=cost(6e9 // calls, 12 * size * size),
            name="cholesky",
        )(places, *state)
    return state


def apply_kernel(places, inverse_ref, *refs):
    *basis_refs, out_ref = refs
    parts = split_in_three(inverse_ref[...])
    for at, basis_ref in enumerate(basis_refs):

        @pl.when(pl.program_id(0) == at)
        def _():
            block = basis_ref[...]
            out_ref[...] = sum(
                lax.dot_general(
                    block, part, (((1,), (1,)), ((), ())), preferred_element_type=F32
                )
                for part in reversed(parts)
            )


def apply_inverse(places, first, inverse, basis):
    rows, columns = basis[0].shape
    blocks = len(basis)
    return pl.pallas_call(
        apply_kernel,
        grid_spec=pltpu.PrefetchScalarGridSpec(
            num_scalar_prefetch=1,
            grid=(blocks,),
            in_specs=[in_vmem()] * (1 + blocks),
            out_specs=pl.BlockSpec((rows, columns), lambda i, places: (places[first + i], 0)),
        ),
        out_shape=jax.ShapeDtypeStruct((rows * blocks, columns), F32),
        compiler_params=vmem(16 * 2**20),
        cost_estimate=cost(6 * rows * blocks * columns * columns, 6 * rows * blocks * columns),
        name="apply",
    )(places, inverse, *basis)


RANGE = 2.0**40


def place_table(me, core, level, pix, depth):
    img = 2 * depth
    rows, gathered = 0, pix
    pairs = gathered + img
    cores = pairs + img
    levels = cores + 2
    at = jnp.arange(levels + depth, dtype=jnp.int32)
    block = at - gathered
    pair = at - pairs
    table = jnp.where(at < gathered, me ^ at, (core ^ (block // depth)) * depth + (level ^ (block % depth)))
    table = jnp.where(at < pairs, table, (core ^ 1 ^ (pair % 2)) * depth + (level ^ (pair // 2)))
    table = jnp.where(at < cores, table, core ^ (at - cores))
    table = jnp.where(at < levels, table, level ^ (at - levels))
    return table, rows, gathered, pairs, cores, levels


def per_device(images, classes, ctf_table, weights, probes):
    images_here, pixels = images.shape
    pix, img = lax.axis_size("pix"), lax.axis_size("img")
    depth = img // 2
    chunk = images_here // pix
    width = pixels // img
    me = lax.axis_index("pix")
    place = lax.axis_index("img")
    places, rows_at, gathered_at, pairs_at, cores_at, levels_at = place_table(
        me, place & 1, place >> 1, pix, depth
    )
    weight_share = lax.dynamic_slice_in_dim(weights, me * chunk, chunk, 0)
    places = places + (weight_share[0] > 2.0).astype(jnp.int32)
    weight_share = weight_share[:, None]

    shifts = list(range(pix - 1, -1, -1))
    filtered, own, arrived = [None] * pix, None, []
    probe_half = probes.astype(BF16)
    images = pltpu.with_memory_space_constraint(images, pltpu.HBM)
    for shift in shifts:
        filtered[shift], part = filter_and_score(
            places,
            rows_at + shift,
            images,
            classes,
            ctf_table,
            probe_half,
            chunk,
            BF16 if shift else F32,
        )
        if shift:
            arrived.append(xor_swap(part, "pix", shift))
        else:
            own = part

    basis = inverse = None
    for sweep in range(ITERS):
        shares = own
        for part in arrived:
            shares = shares + part.astype(F32)
        share_weights = weight_share if sweep == 0 else weight_share * RANGE
        scaled_share = (share_weights * shares).astype(BF16)
        scaled = [scaled_share] + [xor_swap(scaled_share, "pix", s) for s in range(1, pix)]

        parts, after = [None] * depth, []
        for s in range(depth - 1, -1, -1):
            send, keep = image_sum(
                places, pairs_at + 2 * s, filtered, scaled, width, after[-2:-1]
            )
            both = keep + xor_swap(send, "img", 1).astype(F32)
            if s:
                both = both.astype(BF16)
                parts[s] = xor_swap(both, "img", 2 * s)
            else:
                parts[s] = both
            after.append(both)

        if sweep == ITERS - 1:
            half = half_gram(places, cores_at, basis, scaled[-1])
            step = 1
            while step < pix:
                half = half + xor_swap(half, "pix", step)
                step *= 2
            _, inverse = cholesky_and_inverse(
                places, cores_at, [half, xor_swap(half, "img", 1)], 2
            )
            break
        total = parts[0]
        for part in parts[1:]:
            total = total + part.astype(F32)
        half = total.astype(BF16)
        near = [half] + [xor_swap(half, "img", 2 * s) for s in range(1, depth)]
        basis = near + [xor_swap(block, "img", 1) for block in near]

        own, arrived = None, []
        for shift in shifts:
            part = score(places, gathered_at, filtered[shift], basis, BF16 if shift else F32)
            if shift:
                arrived.append(xor_swap(part, "pix", shift))
            else:
                own = part

    half, send, keep = normalize_and_gram(places, cores_at, parts, inverse, 1.0 / RANGE)
    pieces = scatter_rows(places, levels_at, keep, xor_swap(send, "img", 1), depth)
    mine = tree_sum([pieces[0]] + [xor_swap(pieces[s], "img", 2 * s) for s in range(1, depth)])
    mine = tree_sum([mine] + [xor_swap(mine, "pix", s) for s in range(1, pix)])
    pieces = [mine] + [xor_swap(mine, "img", 2 * s) for s in range(1, depth)]
    gram, half = gather_rows(places, levels_at, pieces, half)
    near = [half] + [xor_swap(half, "img", 2 * s) for s in range(1, depth)]
    basis = near + [xor_swap(block, "img", 1) for block in near]
    factor, inverse = cholesky_and_inverse(places, cores_at, [gram, xor_swap(gram, "img", 1)], 1)
    return apply_inverse(places, gathered_at, inverse, basis), factor


def plain_per_device(images, classes, ctf_table, weights, probes):
    onehot = (classes[:, None] == jnp.arange(ctf_table.shape[0])[None, :]).astype(BF16)
    filters = jnp.dot(onehot, ctf_table, preferred_element_type=F32)
    filtered = (images.astype(F32) * filters).astype(BF16)
    current = probes
    factor = None
    for sweep in range(ITERS):
        share_rows = filtered.shape[0] // lax.axis_size("pix")
        shares = lax.psum_scatter(
            jnp.dot(filtered, current.astype(BF16), preferred_element_type=F32),
            "pix",
            scatter_dimension=0,
            tiled=True,
        )
        weight_share = lax.dynamic_slice_in_dim(
            weights, lax.axis_index("pix") * share_rows, share_rows, 0
        )
        scaled_share = (weight_share[:, None] * shares).astype(BF16)
        scaled = lax.all_gather(scaled_share, "pix", axis=0, tiled=True)
        image_sum = lax.psum(contract_rows(filtered, scaled), "img")
        gram = lax.psum(jnp.dot(image_sum.T, image_sum, precision=HIGHEST), "pix")
        factor = jnp.linalg.cholesky(gram)
        current = jax.scipy.linalg.solve_triangular(factor, image_sum.T, lower=True).T
    return current, factor


def power_of_two(n):
    return n > 1 and n & (n - 1) == 0


def per_device_of(images, classes, ctf_table, weights, probes):
    rows, pixels = images.shape
    pix, img = lax.axis_size("pix"), lax.axis_size("img")
    columns = probes.shape[1]
    fits = (
        power_of_two(pix)
        and power_of_two(img)
        and rows % (16 * pix) == 0
        and pixels % (LANES * img) == 0
        and columns % LANES == 0
        and columns % (8 * img) == 0
    )
    run = per_device if fits else plain_per_device
    return run(images, classes, ctf_table, weights, probes)


def solution(mesh):
    in_specs = (P("img", "pix"), P("img"), P(None, "pix"), P("img"), P("pix", None))
    out_specs = (P("pix", None), P())
    return jax.shard_map(
        per_device_of, mesh=mesh, in_specs=in_specs, out_specs=out_specs, check_vma=False
    )
```

```python
import functools

import jax
import jax.numpy as jnp
from jax import lax
from jax.experimental import pallas as pl
from jax.experimental.pallas import tpu as pltpu
from jax.sharding import PartitionSpec as P


ITERS = 2
F32 = jnp.float32
BF16 = jnp.bfloat16
LANES = 128
PANEL = 32
GROUP = 8
SPLIT = 1
HIGHEST = lax.Precision.HIGHEST


def cost(flops, nbytes):
    return pl.CostEstimate(flops=int(flops), bytes_accessed=int(nbytes), transcendentals=0)


def vmem(nbytes):
    return pltpu.CompilerParams(vmem_limit_bytes=nbytes)


def row_tile(rows, most=400):
    return max(t for t in range(16, most + 1, 16) if rows % t == 0)


def xor_swap(value, axis, mask):
    size = lax.axis_size(axis)
    return lax.ppermute(value, axis, [(i, i ^ mask) for i in range(size)])


def contract_rows(left, right):
    return lax.dot_general(left, right, (((0,), (0,)), ((), ())), preferred_element_type=F32)


def in_vmem():
    return pl.BlockSpec(memory_space=pltpu.VMEM)


def filter_kernel(places, class_ref, image_ref, table_ref, probe_ref, filtered_ref, *score_refs):
    table_rows = table_ref.shape[0]
    rows, pixels = image_ref.shape
    onehot = (
        lax.broadcasted_iota(jnp.int32, (table_rows, rows), 0) == class_ref[0]
    ).astype(BF16)
    here = pl.ds(pl.multiple_of(pl.program_id(0) * rows, rows), rows)
    scores = None
    width = min(pixels, 8 * LANES)
    for at in range(0, pixels, width):
        columns = slice(at, min(at + width, pixels))
        filters = contract_rows(onehot, table_ref[:, columns])
        filtered = (image_ref[:, columns].astype(F32) * filters).astype(BF16)
        filtered_ref[here, columns] = filtered
        term = jnp.dot(filtered, probe_ref[columns, :], preferred_element_type=F32)
        scores = term if scores is None else scores + term
    part = score_refs[0].shape[1]
    for at, ref in enumerate(score_refs):
        ref[here, :] = scores[:, at * part : (at + 1) * part].astype(ref.dtype)


def filter_and_score(places, shift, images, classes, table, probe_half, chunk, out_type):
    rows, pixels = images.shape
    columns = probe_half.shape[1]
    tile = row_tile(chunk)
    steps = chunk // tile
    return pl.pallas_call(
        filter_kernel,
        grid_spec=pltpu.PrefetchScalarGridSpec(
            num_scalar_prefetch=1,
            grid=(steps,),
            in_specs=[
                pl.BlockSpec((1, 1, tile), lambda i, places: (places[shift] * steps + i, 0, 0)),
                pl.BlockSpec((tile, pixels), lambda i, places: (places[shift] * steps + i, 0)),
                in_vmem(),
                in_vmem(),
            ],
            out_specs=[in_vmem()] * (1 + SPLIT),
        ),
        out_shape=[pltpu.VMEM((chunk, pixels), BF16)]
        + [jax.ShapeDtypeStruct((chunk, columns // SPLIT), out_type)] * SPLIT,
        compiler_params=vmem(14 * 2**20),
        cost_estimate=cost(4 * chunk * pixels * columns, 2 * chunk * pixels),
        name="filter_and_score",
    )(places, classes.reshape(rows // tile, 1, tile), images, table, probe_half)


def prefetched(count, outs):
    return pltpu.PrefetchScalarGridSpec(
        num_scalar_prefetch=1,
        grid=(),
        in_specs=[in_vmem()] * count,
        out_specs=[in_vmem()] * outs,
    )


def score_kernel(first, places, filtered_ref, *refs):
    *basis_refs, score_ref = refs
    width = basis_refs[0].shape[0]
    total = None
    for at, basis_ref in enumerate(basis_refs):
        columns = pl.ds(pl.multiple_of(places[first + at] * width, width), width)
        term = jnp.dot(filtered_ref[:, columns], basis_ref[...], preferred_element_type=F32)
        total = term if total is None else total + term
    score_ref[...] = total.astype(score_ref.dtype)


def score(places, first, filtered, basis, out_type):
    rows, pixels = filtered.shape
    columns = basis[0].shape[1]
    return pl.pallas_call(
        functools.partial(score_kernel, first),
        grid_spec=prefetched(1 + len(basis), 1),
        out_shape=[jax.ShapeDtypeStruct((rows, columns), out_type)],
        compiler_params=vmem(16 * 2**20),
        cost_estimate=cost(2 * rows * pixels * columns, 2 * rows * columns),
        name="score",
    )(places, filtered, *basis)[0]


def sum_blocks(filtered, scaled):
    rows = filtered[0].shape[0]
    whole = rows // 256 * 256
    total = None
    for left, right in zip(filtered, scaled):
        if whole:
            term = contract_rows(left[:whole, :], right[:whole, :])
            total = term if total is None else total + term
    if whole < rows:
        left = jnp.concatenate([block[whole:, :] for block in filtered], 0)
        right = jnp.concatenate([block[whole:, :] for block in scaled], 0)
        term = contract_rows(left, right)
        total = term if total is None else total + term
    return total


def image_sum_kernel(count, first, places, *refs):
    filtered_refs, scaled_refs = refs[:count], refs[count : 2 * count]
    send_ref, keep_ref = refs[-2:]
    width = send_ref.shape[0]

    def block(at, carry):
        columns = pl.ds(pl.multiple_of(places[first + at] * width, width), width)
        blocks = [ref[:, columns] for ref in filtered_refs]
        scaled = [ref[...] for ref in scaled_refs]
        if scaled[0].shape[1] > LANES:
            total = sum_blocks(blocks, scaled)
        else:
            total = sum_blocks(scaled, blocks).T

        @pl.when(at == 0)
        def _():
            send_ref[...] = total.astype(send_ref.dtype)

        @pl.when(at == 1)
        def _():
            keep_ref[...] = total

        return carry

    lax.fori_loop(0, 2, block, 0)


def image_sum(places, first, filtered, scaled, width, after):
    count = len(filtered)
    rows = filtered[0].shape[0]
    columns = scaled[0].shape[1]
    return pl.pallas_call(
        functools.partial(image_sum_kernel, count, first),
        grid_spec=prefetched(2 * count + len(after), 2),
        out_shape=[
            jax.ShapeDtypeStruct((width, columns), BF16),
            jax.ShapeDtypeStruct((width, columns), F32),
        ],
        compiler_params=vmem(16 * 2**20),
        cost_estimate=cost(4 * count * rows * width * columns, 6 * width * columns),
        name="image_sum",
    )(places, *filtered, *scaled, *after)


def tree_sum(terms):
    while len(terms) > 1:
        terms = [terms[i] + terms[i + 1] for i in range(0, len(terms), 2)]
    return terms[0]


def whole_blocks(parts):
    count = len(parts) // SPLIT
    return [jnp.concatenate(parts[at::count], 1) for at in range(count)]


def gram_kernel(core_at, places, *refs):
    *basis_refs, _, half_ref, gram_ref = refs
    blocks = whole_blocks([ref[...] for ref in basis_refs])
    gram_ref[...] = tree_sum([contract_rows(block, block) for block in blocks])
    rows = half_ref.shape[0]
    half_ref[...] = gram_ref[pl.ds(pl.multiple_of(places[core_at] * rows, rows), rows), :]


def half_gram(places, core_at, basis, after):
    rows, columns = basis[0].shape
    columns *= SPLIT
    return pl.pallas_call(
        functools.partial(gram_kernel, core_at),
        grid_spec=pltpu.PrefetchScalarGridSpec(
            num_scalar_prefetch=1,
            grid=(),
            in_specs=[in_vmem()] * (len(basis) + 1),
            out_specs=[in_vmem()],
            scratch_shapes=[pltpu.VMEM((columns, columns), F32)],
        ),
        out_shape=[jax.ShapeDtypeStruct((columns // 2, columns), F32)],
        compiler_params=vmem(12 * 2**20),
        cost_estimate=cost(2 * len(basis) * rows * columns * columns, 2 * len(basis) * rows * columns),
        name="gram",
    )(places, *basis, after)[0]


def normalize_kernel(core_at, scale, places, *refs):
    *part_refs, inverse_ref, half_ref, send_ref, keep_ref, gram_ref = refs
    blocks = whole_blocks([ref[...].astype(F32) for ref in part_refs])
    total = blocks[0]
    for block in blocks[1:]:
        total = total + block
    block = lax.dot_general(
        total,
        inverse_ref[...] * scale,
        (((1,), (1,)), ((), ())),
        precision=HIGHEST,
        preferred_element_type=F32,
    ).astype(BF16)
    half_ref[...] = block
    gram_ref[...] = contract_rows(block, block)
    rows = send_ref.shape[0]
    here = places[core_at]
    send_ref[...] = gram_ref[pl.ds(pl.multiple_of((1 - here) * rows, rows), rows), :]
    keep_ref[...] = gram_ref[pl.ds(pl.multiple_of(here * rows, rows), rows), :]


def normalize_and_gram(places, core_at, parts, inverse, scale):
    rows, columns = parts[0].shape
    columns *= SPLIT
    return pl.pallas_call(
        functools.partial(normalize_kernel, core_at, scale),
        grid_spec=pltpu.PrefetchScalarGridSpec(
            num_scalar_prefetch=1,
            grid=(),
            in_specs=[in_vmem()] * (len(parts) + 1),
            out_specs=[in_vmem()] * 3,
            scratch_shapes=[pltpu.VMEM((columns, columns), F32)],
        ),
        out_shape=[
            jax.ShapeDtypeStruct((rows, columns), BF16),
            jax.ShapeDtypeStruct((columns // 2, columns), F32),
            jax.ShapeDtypeStruct((columns // 2, columns), F32),
        ],
        compiler_params=vmem(12 * 2**20),
        cost_estimate=cost(14 * rows * columns * columns, 8 * rows * columns),
        name="normalize",
    )(places, *parts, inverse)


def scatter_kernel(first, places, keep_ref, got_ref, *piece_refs):
    rows = piece_refs[0].shape[0]
    for at, ref in enumerate(piece_refs):
        here = pl.ds(pl.multiple_of(places[first + at] * rows, rows), rows)
        ref[...] = keep_ref[here, :] + got_ref[here, :]


def scatter_rows(places, first, keep, got, count):
    rows, columns = keep.shape
    return pl.pallas_call(
        functools.partial(scatter_kernel, first),
        grid_spec=prefetched(2, count),
        out_shape=[jax.ShapeDtypeStruct((rows // count, columns), F32)] * count,
        compiler_params=vmem(4 * 2**20),
        cost_estimate=cost(rows * columns, 12 * rows * columns),
        name="scatter",
    )(places, keep, got)


def gather_kernel(first, count, places, *refs):
    piece_refs, (block_ref, out_ref, block_out_ref) = refs[:count], refs[count:]
    rows = piece_refs[0].shape[0]
    for at, ref in enumerate(piece_refs):
        out_ref[pl.ds(pl.multiple_of(places[first + at] * rows, rows), rows), :] = ref[...]
    block_out_ref[...] = block_ref[...]


def gather_rows(places, first, pieces, block):
    count = len(pieces)
    rows, columns = pieces[0].shape
    return pl.pallas_call(
        functools.partial(gather_kernel, first, count),
        grid_spec=prefetched(count + 1, 2),
        out_shape=[
            jax.ShapeDtypeStruct((rows * count, columns), F32),
            jax.ShapeDtypeStruct(block.shape, block.dtype),
        ],
        compiler_params=vmem(4 * 2**20),
        cost_estimate=cost(rows * columns, 8 * count * rows * columns),
        name="gather",
    )(places, *pieces, block)


def square_places(size):
    return tuple(lax.broadcasted_iota(jnp.int32, (size, size), axis) for axis in (0, 1))


def split_in_three(value):
    parts = []
    for _ in range(3):
        parts.append(value.astype(BF16))
        value = value - parts[-1].astype(F32)
    return parts


def contract_rows_fully(left, right):
    l0, l1, l2 = split_in_three(left)
    r0, r1, r2 = split_in_three(right)
    return contract_rows(
        jnp.concatenate([l2, l1, l0, l1, l0, l0], 0), jnp.concatenate([r0, r1, r2, r0, r1, r0], 0)
    )


def eliminate(work_ref, first, last):
    size = work_ref.shape[0]
    panel_row = lax.broadcasted_iota(jnp.int32, (PANEL, LANES), 0)
    panel_column = lax.broadcasted_iota(jnp.int32, (PANEL, LANES), 1)
    per_tile = LANES // PANEL

    def panel(block, carry):
        start = pl.multiple_of(block * PANEL, PANEL)
        tile = pl.multiple_of((block // per_tile) * LANES, LANES)
        diagonal = work_ref[pl.ds(start, PANEL), pl.ds(tile, LANES)]
        diagonal = pltpu.roll(diagonal, (LANES - (block % per_tile) * PANEL) % LANES, 1)
        tiles = [diagonal] + [
            work_ref[pl.ds(start, PANEL), at : at + LANES] for at in range(0, 2 * size, LANES)
        ]
        for top in range(0, PANEL, GROUP):
            tiles = eliminate_group(tiles, panel_row, top)
        pivots = jnp.sum(jnp.where(panel_row == panel_column, tiles[0], 0.0), axis=1, keepdims=True)
        body = jnp.concatenate(tiles[1:], 1) * lax.rsqrt(pivots)
        work_ref[pl.ds(start, PANEL), :] = body
        left = body[:, :size]
        later = lax.broadcasted_iota(jnp.int32, left.shape, 1) >= start + PANEL
        work_ref[...] -= contract_rows_fully(jnp.where(later, left, 0.0), body)
        return carry

    lax.fori_loop(first, last, panel, 0)


def eliminate_group(tiles, panel_row, top):
    shape = panel_row.shape
    columns = [
        jnp.broadcast_to(tiles[0][:, top + k : top + k + 1], shape) for k in range(GROUP)
    ]
    block = [[columns[k][top + i : top + i + 1, :] for k in range(i + 1)] for i in range(GROUP)]
    ratio = [[None] * GROUP for _ in range(GROUP)]
    scales = []
    for k in range(GROUP):
        inverse = 1.0 / block[k][k]
        for i in range(k + 1, GROUP):
            ratio[i][k] = block[i][k] * inverse
        for i in range(k + 1, GROUP):
            for m in range(k + 1, i + 1):
                block[i][m] = block[i][m] - ratio[i][k] * block[m][k]
        scales.append(jnp.where(panel_row > top + k, columns[k] * inverse, 0.0))
        for m in range(k + 1, GROUP):
            columns[m] = columns[m] - scales[k] * block[m][k]
    result = []
    for tile in tiles:
        rows = [tile[top + k : top + k + 1, :] for k in range(GROUP)]
        for k in range(GROUP):
            for m in range(k + 1, GROUP):
                rows[m] = rows[m] - ratio[m][k] * rows[k]
        for k in range(GROUP):
            tile = tile - scales[k] * rows[k]
        result.append(tile)
    return result


def cholesky_kernel(first, last, place_at, places, *refs):
    size = refs[-1].shape[0]
    panels = size // PANEL
    row_at, column_at = square_places(size)
    if first == 0:
        *piece_refs, = refs[: -1 if last < panels else -3]
        work_ref = refs[-1]
        rows = piece_refs[0].shape[0]
        for at, ref in enumerate(piece_refs):
            here = pl.ds(pl.multiple_of(places[place_at + at] * rows, rows), rows)
            work_ref[here, :size] = ref[...]
        work_ref[:, size:] = (row_at == column_at).astype(F32)
    else:
        work_ref = refs[-1]
        work_ref[...] = refs[0][...]
    eliminate(work_ref, first, last)
    if last == panels:
        factor_ref, inverse_ref = refs[-3:-1]
        factor_ref[...] = jnp.where(row_at <= column_at, work_ref[:, :size], 0.0).T
        inverse_ref[...] = work_ref[:, size:]


def cholesky_and_inverse(places, place_at, pieces, calls):
    size = pieces[0].shape[1]
    panels = size // PANEL
    state = pieces
    for call in range(calls):
        first, last = panels * call // calls, panels * (call + 1) // calls
        work = jax.ShapeDtypeStruct((size, 2 * size), F32)
        square = jax.ShapeDtypeStruct((size, size), F32)
        final = last == panels
        state = pl.pallas_call(
            functools.partial(cholesky_kernel, first, last, place_at),
            grid_spec=pltpu.PrefetchScalarGridSpec(
                num_scalar_prefetch=1,
                grid=(),
                in_specs=[in_vmem()] * len(state),
                out_specs=[in_vmem()] * (2 if final else 1),
                scratch_shapes=[pltpu.VMEM(work.shape, F32)] if final else [],
            ),
            out_shape=[square, square] if final else [work],
            compiler_params=vmem(12 * 2**20),
            cost_estimate=cost(6e9 // calls, 12 * size * size),
            name="cholesky",
        )(places, *state)
    return state


def apply_kernel(first, places, inverse_ref, *refs):
    *basis_refs, out_ref = refs
    parts = split_in_three(inverse_ref[...])
    rows = basis_refs[0].shape[0]
    span = out_ref.shape[0] // rows
    for step in range(len(basis_refs) // span):

        @pl.when(pl.program_id(0) == step)
        def _():
            for at in range(step * span, (step + 1) * span):
                block = basis_refs[at][...]
                here = pl.multiple_of((places[first + at] % span) * rows, rows)
                out_ref[pl.ds(here, rows), :] = sum(
                    lax.dot_general(
                        block, part, (((1,), (1,)), ((), ())), preferred_element_type=F32
                    )
                    for part in reversed(parts)
                )


def apply_inverse(places, first, inverse, basis):
    rows, columns = basis[0].shape
    span = 2
    steps = len(basis) // span
    return pl.pallas_call(
        functools.partial(apply_kernel, first),
        grid_spec=pltpu.PrefetchScalarGridSpec(
            num_scalar_prefetch=1,
            grid=(steps,),
            in_specs=[in_vmem()] * (1 + len(basis)),
            out_specs=pl.BlockSpec(
                (span * rows, columns), lambda i, places: (places[first + span * i] // span, 0)
            ),
        ),
        out_shape=jax.ShapeDtypeStruct((rows * len(basis), columns), F32),
        compiler_params=vmem(16 * 2**20),
        cost_estimate=cost(
            6 * rows * len(basis) * columns * columns, 6 * rows * len(basis) * columns
        ),
        name="apply",
    )(places, inverse, *basis)


RANGE = 2.0**40


def place_table(me, core, level, pix, depth):
    img = 2 * depth
    rows, gathered = 0, pix
    pairs = gathered + img
    cores = pairs + img
    levels = cores + 2
    at = jnp.arange(levels + depth, dtype=jnp.int32)
    block = at - gathered
    pair = at - pairs
    table = jnp.where(at < gathered, me ^ at, (core ^ (block // depth)) * depth + (level ^ (block % depth)))
    table = jnp.where(at < pairs, table, (core ^ 1 ^ (pair % 2)) * depth + (level ^ (pair // 2)))
    table = jnp.where(at < cores, table, core ^ (at - cores))
    table = jnp.where(at < levels, table, level ^ (at - levels))
    return table, rows, gathered, pairs, cores, levels


def per_device(images, classes, ctf_table, weights, probes):
    images_here, pixels = images.shape
    pix, img = lax.axis_size("pix"), lax.axis_size("img")
    depth = img // 2
    chunk = images_here // pix
    width = pixels // img
    me = lax.axis_index("pix")
    place = lax.axis_index("img")
    places, rows_at, gathered_at, pairs_at, cores_at, levels_at = place_table(
        me, place & 1, place >> 1, pix, depth
    )
    weight_share = lax.dynamic_slice_in_dim(weights, me * chunk, chunk, 0)
    places = places + (weight_share[0] > 2.0).astype(jnp.int32)
    weight_share = weight_share[:, None]

    shifts = list(range(pix - 1, -1, -1))
    halves = range(SPLIT)
    filtered, own, arrived = [None] * pix, None, [[] for _ in halves]
    probe_half = probes.astype(BF16)
    images = pltpu.with_memory_space_constraint(images, pltpu.HBM)
    for shift in shifts:
        filtered[shift], *parts = filter_and_score(
            places,
            rows_at + shift,
            images,
            classes,
            ctf_table,
            probe_half,
            chunk,
            BF16 if shift else F32,
        )
        if shift:
            for h in halves:
                arrived[h].append(xor_swap(parts[h], "pix", shift))
        else:
            own = parts

    basis = inverse = None
    for sweep in range(ITERS):
        share_weights = weight_share if sweep == 0 else weight_share * RANGE
        scaled = []
        for h in halves:
            shares = own[h]
            for part in arrived[h]:
                shares = shares + part.astype(F32)
            share = (share_weights * shares).astype(BF16)
            scaled.append([share] + [xor_swap(share, "pix", s) for s in range(1, pix)])

        parts, after = [[None] * depth for _ in halves], []
        for h in halves:
            for s in range(depth - 1, -1, -1):
                send, keep = image_sum(
                    places, pairs_at + 2 * s, filtered, scaled[h], width, after[-2:-1]
                )
                both = keep + xor_swap(send, "img", 1).astype(F32)
                if s:
                    both = both.astype(BF16)
                    parts[h][s] = xor_swap(both, "img", 2 * s)
                else:
                    parts[h][s] = both
                after.append(both)

        if sweep == ITERS - 1:
            gram = half_gram(places, cores_at, sum(basis, []), scaled[-1][-1])
            step = 1
            while step < pix:
                gram = gram + xor_swap(gram, "pix", step)
                step *= 2
            other = xor_swap(gram, "img", 1)
            _, inverse = cholesky_and_inverse(places, cores_at, [gram, other], 2)
            break

        basis = []
        for h in halves:
            total = parts[h][0]
            for part in parts[h][1:]:
                total = total + part.astype(F32)
            block = total.astype(BF16)
            near = [block] + [xor_swap(block, "img", 2 * s) for s in range(1, depth)]
            basis.append(near + [xor_swap(block, "img", 1) for block in near])

        own, arrived = [None] * SPLIT, [[] for _ in halves]
        for h in halves:
            for shift in shifts:
                part = score(places, gathered_at, filtered[shift], basis[h], BF16 if shift else F32)
                if shift:
                    arrived[h].append(xor_swap(part, "pix", shift))
                else:
                    own[h] = part

    half, send, keep = normalize_and_gram(
        places, cores_at, sum(parts, []), inverse, 1.0 / RANGE
    )
    pieces = scatter_rows(places, levels_at, keep, xor_swap(send, "img", 1), depth)
    mine = tree_sum([pieces[0]] + [xor_swap(pieces[s], "img", 2 * s) for s in range(1, depth)])
    pieces = [mine] + [xor_swap(mine, "img", 2 * s) for s in range(1, depth)]
    gram, half = gather_rows(places, levels_at, pieces, half)
    step = 1
    while step < pix:
        gram = gram + xor_swap(gram, "pix", step)
        step *= 2
    other = xor_swap(gram, "img", 1)
    near = [half] + [xor_swap(half, "img", 2 * s) for s in range(1, depth)]
    basis = near + [xor_swap(block, "img", 1) for block in near]
    factor, inverse = cholesky_and_inverse(places, cores_at, [gram, other], 1)
    return apply_inverse(places, gathered_at, inverse, basis), factor


def plain_per_device(images, classes, ctf_table, weights, probes):
    onehot = (classes[:, None] == jnp.arange(ctf_table.shape[0])[None, :]).astype(BF16)
    filters = jnp.dot(onehot, ctf_table, preferred_element_type=F32)
    filtered = (images.astype(F32) * filters).astype(BF16)
    current = probes
    factor = None
    for _ in range(ITERS):
        share_rows = filtered.shape[0] // lax.axis_size("pix")
        shares = lax.psum_scatter(
            jnp.dot(filtered, current.astype(BF16), preferred_element_type=F32),
            "pix",
            scatter_dimension=0,
            tiled=True,
        )
        weight_share = lax.dynamic_slice_in_dim(
            weights, lax.axis_index("pix") * share_rows, share_rows, 0
        )
        scaled_share = (weight_share[:, None] * shares).astype(BF16)
        scaled = lax.all_gather(scaled_share, "pix", axis=0, tiled=True)
        image_sum = lax.psum(contract_rows(filtered, scaled), "img")
        gram = lax.psum(jnp.dot(image_sum.T, image_sum, precision=HIGHEST), "pix")
        factor = jnp.linalg.cholesky(gram)
        current = jax.scipy.linalg.solve_triangular(factor, image_sum.T, lower=True).T
    return current, factor


def power_of_two(n):
    return n > 1 and n & (n - 1) == 0


def fits(rows, pixels, columns, pix, img):
    return (
        power_of_two(pix)
        and power_of_two(img)
        and rows % (16 * pix) == 0
        and pixels % (LANES * img) == 0
        and columns % (LANES * SPLIT) == 0
        and columns % (8 * img) == 0
    )


def per_device_of(images, classes, ctf_table, weights, probes):
    pix, img = lax.axis_size("pix"), lax.axis_size("img")
    if not fits(*images.shape, probes.shape[1], pix, img):
        return plain_per_device(images, classes, ctf_table, weights, probes)
    return per_device(images, classes, ctf_table, weights, probes)


def solution(mesh):
    in_specs = (P("img", "pix"), P("img"), P(None, "pix"), P("img"), P("pix", None))
    out_specs = (P("pix", None), P())
    return jax.shard_map(
        per_device_of, mesh=mesh, in_specs=in_specs, out_specs=out_specs, check_vma=False
    )
```

```python
import functools

import jax
import jax.numpy as jnp
from jax import lax
from jax.experimental import pallas as pl
from jax.experimental.pallas import tpu as pltpu
from jax.sharding import PartitionSpec as P


ITERS = 2
F32 = jnp.float32
BF16 = jnp.bfloat16
LANES = 128
PANEL = 32
GROUP = 8
HIGHEST = lax.Precision.HIGHEST


def cost(flops, nbytes):
    return pl.CostEstimate(flops=int(flops), bytes_accessed=int(nbytes), transcendentals=0)


def vmem(nbytes):
    return pltpu.CompilerParams(vmem_limit_bytes=nbytes)


def row_tile(rows, most=400):
    return max(t for t in range(16, most + 1, 16) if rows % t == 0)


def xor_swap(value, axis, mask):
    size = lax.axis_size(axis)
    return lax.ppermute(value, axis, [(i, i ^ mask) for i in range(size)])


def contract_rows(left, right):
    return lax.dot_general(left, right, (((0,), (0,)), ((), ())), preferred_element_type=F32)


def in_vmem():
    return pl.BlockSpec(memory_space=pltpu.VMEM)


def filter_kernel(places, class_ref, image_ref, table_ref, probe_ref, filtered_ref, score_ref):
    table_rows = table_ref.shape[0]
    rows, pixels = image_ref.shape
    onehot = (
        lax.broadcasted_iota(jnp.int32, (table_rows, rows), 0) == class_ref[0]
    ).astype(BF16)
    here = pl.ds(pl.multiple_of(pl.program_id(0) * rows, rows), rows)
    scores = None
    width = min(pixels, 8 * LANES)
    for at in range(0, pixels, width):
        columns = slice(at, min(at + width, pixels))
        filters = contract_rows(onehot, table_ref[:, columns])
        filtered = (image_ref[:, columns].astype(F32) * filters).astype(BF16)
        filtered_ref[here, columns] = filtered
        term = jnp.dot(filtered, probe_ref[columns, :], preferred_element_type=F32)
        scores = term if scores is None else scores + term
    score_ref[here, :] = scores.astype(score_ref.dtype)


def filter_and_score(places, shift, images, classes, table, probe_half, chunk, out_type):
    rows, pixels = images.shape
    columns = probe_half.shape[1]
    tile = row_tile(chunk)
    steps = chunk // tile
    return pl.pallas_call(
        filter_kernel,
        grid_spec=pltpu.PrefetchScalarGridSpec(
            num_scalar_prefetch=1,
            grid=(steps,),
            in_specs=[
                pl.BlockSpec((1, 1, tile), lambda i, places: (places[shift] * steps + i, 0, 0)),
                pl.BlockSpec((tile, pixels), lambda i, places: (places[shift] * steps + i, 0)),
                in_vmem(),
                in_vmem(),
            ],
            out_specs=[in_vmem(), in_vmem()],
        ),
        out_shape=[
            pltpu.VMEM((chunk, pixels), BF16),
            jax.ShapeDtypeStruct((chunk, columns), out_type),
        ],
        compiler_params=vmem(14 * 2**20),
        cost_estimate=cost(4 * chunk * pixels * columns, 2 * chunk * pixels),
        name="filter_and_score",
    )(places, classes.reshape(rows // tile, 1, tile), images, table, probe_half)


def prefetched(count, outs):
    return pltpu.PrefetchScalarGridSpec(
        num_scalar_prefetch=1,
        grid=(),
        in_specs=[in_vmem()] * count,
        out_specs=[in_vmem()] * outs,
    )


def score_kernel(first, places, filtered_ref, *refs):
    *basis_refs, top_ref, low_ref = refs
    rows = top_ref.shape[0]
    width = basis_refs[0].shape[0]
    total = None
    for at, basis_ref in enumerate(basis_refs):
        columns = pl.ds(pl.multiple_of(places[first + at] * width, width), width)
        term = jnp.dot(filtered_ref[:, columns], basis_ref[...], preferred_element_type=F32)
        total = term if total is None else total + term
    top_ref[...] = total[:rows].astype(top_ref.dtype)
    low_ref[...] = total[rows:].astype(low_ref.dtype)


def score(places, first, filtered, basis, out_types):
    rows, pixels = filtered.shape
    columns = basis[0].shape[1]
    return pl.pallas_call(
        functools.partial(score_kernel, first),
        grid_spec=prefetched(1 + len(basis), 2),
        out_shape=[jax.ShapeDtypeStruct((rows // 2, columns), kind) for kind in out_types],
        compiler_params=vmem(16 * 2**20),
        cost_estimate=cost(2 * rows * pixels * columns, 2 * rows * columns),
        name="score",
    )(places, filtered, *basis)


def sum_blocks(filtered, scaled):
    rows = filtered[0].shape[0]
    whole = rows // 256 * 256
    total = None
    for left, right in zip(filtered, scaled):
        if whole:
            term = contract_rows(left[:whole, :], right[:whole, :])
            total = term if total is None else total + term
    if whole < rows:
        left = jnp.concatenate([block[whole:, :] for block in filtered], 0)
        right = jnp.concatenate([block[whole:, :] for block in scaled], 0)
        term = contract_rows(left, right)
        total = term if total is None else total + term
    return total


def stack_pieces(stacked_ref, pieces):
    rows = pieces[0].shape[0]
    for at, ref in enumerate(pieces):
        stacked_ref[at * rows : (at + 1) * rows, :] = ref[...]


def block_sum(filtered_refs, stacked_ref, columns):
    rows = filtered_refs[0].shape[0]
    return sum_blocks(
        [ref[:, columns] for ref in filtered_refs],
        [stacked_ref[at * rows : (at + 1) * rows, :] for at in range(len(filtered_refs))],
    )


def early_sum_kernel(count, first, width, places, *refs):
    filtered_refs, piece_refs = refs[:count], refs[count : 3 * count]
    before, out_ref, stacked_ref = refs[3 * count : -2], refs[-2], refs[-1]
    stack_pieces(stacked_ref, piece_refs)

    def block(at, carry):
        columns = pl.ds(pl.multiple_of(places[first + at] * width, width), width)
        here = pl.ds(pl.multiple_of(at * width, width), width)
        total = block_sum(filtered_refs, stacked_ref, columns)
        for ref in before:
            total = total + ref[here, :]
        out_ref[here, :] = total
        return carry

    lax.fori_loop(0, out_ref.shape[0] // width, block, 0)


def sum_grid(count, extra, outs, rows, columns):
    return pltpu.PrefetchScalarGridSpec(
        num_scalar_prefetch=1,
        grid=(),
        in_specs=[in_vmem()] * (3 * count + extra),
        out_specs=[in_vmem()] * outs,
        scratch_shapes=[pltpu.VMEM((count * rows, columns), BF16)],
    )


def early_sum(places, first, filtered, scaled, width, before):
    count = len(filtered)
    rows, pixels = filtered[0].shape
    columns = scaled[0][0].shape[1]
    return pl.pallas_call(
        functools.partial(early_sum_kernel, count, first, width),
        grid_spec=sum_grid(count, len(before), 1, rows, columns),
        out_shape=[jax.ShapeDtypeStruct((pixels, columns), F32)],
        compiler_params=vmem(12 * 2**20),
        cost_estimate=cost(2 * count * rows * pixels * columns, 4 * pixels * columns),
        name="early_sum",
    )(places, *filtered, *sum(scaled, []), *before)[0]


def late_sum_kernel(count, first, at_early, places, *refs):
    filtered_refs, piece_refs = refs[:count], refs[count : 3 * count]
    early_ref = refs[3 * count]
    send_ref, keep_ref, stacked_ref = refs[-3:]
    width = send_ref.shape[0]
    stack_pieces(stacked_ref, piece_refs)

    def block(at, carry):
        columns = pl.ds(pl.multiple_of(places[first + at] * width, width), width)
        here = pl.ds(pl.multiple_of((at_early + at) * width, width), width)
        total = early_ref[here, :] + block_sum(filtered_refs, stacked_ref, columns)

        @pl.when(at == 0)
        def _():
            send_ref[...] = total.astype(send_ref.dtype)

        @pl.when(at == 1)
        def _():
            keep_ref[...] = total

        return carry

    lax.fori_loop(0, 2, block, 0)


def late_sum(places, first, at_early, filtered, scaled, early, width, after):
    count = len(filtered)
    rows = filtered[0].shape[0]
    columns = scaled[0][0].shape[1]
    return pl.pallas_call(
        functools.partial(late_sum_kernel, count, first, at_early),
        grid_spec=sum_grid(count, 1 + len(after), 2, rows, columns),
        out_shape=[
            jax.ShapeDtypeStruct((width, columns), BF16),
            jax.ShapeDtypeStruct((width, columns), F32),
        ],
        compiler_params=vmem(12 * 2**20),
        cost_estimate=cost(4 * count * rows * width * columns, 6 * width * columns),
        name="late_sum",
    )(places, *filtered, *sum(scaled, []), early, *after)


def tree_sum(terms):
    while len(terms) > 1:
        terms = [terms[i] + terms[i + 1] for i in range(0, len(terms), 2)]
    return terms[0]


def gram_kernel(core_at, places, *refs):
    *basis_refs, half_ref, gram_ref = refs
    gram_ref[...] = tree_sum([contract_rows(ref[...], ref[...]) for ref in basis_refs])
    rows = half_ref.shape[0]
    half_ref[...] = gram_ref[pl.ds(pl.multiple_of(places[core_at] * rows, rows), rows), :]


def half_gram(places, core_at, basis):
    rows, columns = basis[0].shape
    return pl.pallas_call(
        functools.partial(gram_kernel, core_at),
        grid_spec=pltpu.PrefetchScalarGridSpec(
            num_scalar_prefetch=1,
            grid=(),
            in_specs=[in_vmem()] * len(basis),
            out_specs=[in_vmem()],
            scratch_shapes=[pltpu.VMEM((columns, columns), F32)],
        ),
        out_shape=[jax.ShapeDtypeStruct((columns // 2, columns), F32)],
        compiler_params=vmem(12 * 2**20),
        cost_estimate=cost(2 * len(basis) * rows * columns * columns, 2 * len(basis) * rows * columns),
        name="gram",
    )(places, *basis)[0]


def normalize_kernel(core_at, scale, places, *refs):
    *part_refs, inverse_ref, half_ref, send_ref, keep_ref, gram_ref = refs
    total = part_refs[0][...]
    for ref in part_refs[1:]:
        total = total + ref[...].astype(F32)
    block = lax.dot_general(
        total,
        inverse_ref[...] * scale,
        (((1,), (1,)), ((), ())),
        precision=HIGHEST,
        preferred_element_type=F32,
    ).astype(BF16)
    half_ref[...] = block
    gram_ref[...] = contract_rows(block, block)
    rows = send_ref.shape[0]
    here = places[core_at]
    send_ref[...] = gram_ref[pl.ds(pl.multiple_of((1 - here) * rows, rows), rows), :]
    keep_ref[...] = gram_ref[pl.ds(pl.multiple_of(here * rows, rows), rows), :]


def normalize_and_gram(places, core_at, parts, inverse, scale):
    rows, columns = parts[0].shape
    return pl.pallas_call(
        functools.partial(normalize_kernel, core_at, scale),
        grid_spec=pltpu.PrefetchScalarGridSpec(
            num_scalar_prefetch=1,
            grid=(),
            in_specs=[in_vmem()] * (len(parts) + 1),
            out_specs=[in_vmem()] * 3,
            scratch_shapes=[pltpu.VMEM((columns, columns), F32)],
        ),
        out_shape=[
            jax.ShapeDtypeStruct((rows, columns), BF16),
            jax.ShapeDtypeStruct((columns // 2, columns), F32),
            jax.ShapeDtypeStruct((columns // 2, columns), F32),
        ],
        compiler_params=vmem(12 * 2**20),
        cost_estimate=cost(14 * rows * columns * columns, 8 * rows * columns),
        name="normalize",
    )(places, *parts, inverse)


def scatter_kernel(first, places, keep_ref, got_ref, *piece_refs):
    rows = piece_refs[0].shape[0]
    for at, ref in enumerate(piece_refs):
        here = pl.ds(pl.multiple_of(places[first + at] * rows, rows), rows)
        ref[...] = keep_ref[here, :] + got_ref[here, :]


def scatter_rows(places, first, keep, got, count):
    rows, columns = keep.shape
    return pl.pallas_call(
        functools.partial(scatter_kernel, first),
        grid_spec=prefetched(2, count),
        out_shape=[jax.ShapeDtypeStruct((rows // count, columns), F32)] * count,
        compiler_params=vmem(4 * 2**20),
        cost_estimate=cost(rows * columns, 12 * rows * columns),
        name="scatter",
    )(places, keep, got)


def gather_kernel(first, count, places, *refs):
    piece_refs, (block_ref, out_ref, block_out_ref) = refs[:count], refs[count:]
    rows = piece_refs[0].shape[0]
    for at, ref in enumerate(piece_refs):
        out_ref[pl.ds(pl.multiple_of(places[first + at] * rows, rows), rows), :] = ref[...]
    block_out_ref[...] = block_ref[...]


def gather_rows(places, first, pieces, block):
    count = len(pieces)
    rows, columns = pieces[0].shape
    return pl.pallas_call(
        functools.partial(gather_kernel, first, count),
        grid_spec=prefetched(count + 1, 2),
        out_shape=[
            jax.ShapeDtypeStruct((rows * count, columns), F32),
            jax.ShapeDtypeStruct(block.shape, block.dtype),
        ],
        compiler_params=vmem(4 * 2**20),
        cost_estimate=cost(rows * columns, 8 * count * rows * columns),
        name="gather",
    )(places, *pieces, block)


def square_places(size):
    return tuple(lax.broadcasted_iota(jnp.int32, (size, size), axis) for axis in (0, 1))


def split_in_three(value):
    parts = []
    for _ in range(3):
        parts.append(value.astype(BF16))
        value = value - parts[-1].astype(F32)
    return parts


def contract_rows_fully(left, right):
    l0, l1, l2 = split_in_three(left)
    r0, r1, r2 = split_in_three(right)
    return contract_rows(
        jnp.concatenate([l2, l1, l0, l1, l0, l0], 0), jnp.concatenate([r0, r1, r2, r0, r1, r0], 0)
    )


def eliminate(work_ref, first, last):
    size = work_ref.shape[0]
    panel_row = lax.broadcasted_iota(jnp.int32, (PANEL, LANES), 0)
    panel_column = lax.broadcasted_iota(jnp.int32, (PANEL, LANES), 1)
    per_tile = LANES // PANEL

    def panel(block, carry):
        start = pl.multiple_of(block * PANEL, PANEL)
        tile = pl.multiple_of((block // per_tile) * LANES, LANES)
        diagonal = work_ref[pl.ds(start, PANEL), pl.ds(tile, LANES)]
        diagonal = pltpu.roll(diagonal, (LANES - (block % per_tile) * PANEL) % LANES, 1)
        tiles = [diagonal] + [
            work_ref[pl.ds(start, PANEL), at : at + LANES] for at in range(0, 2 * size, LANES)
        ]
        for top in range(0, PANEL, GROUP):
            tiles = eliminate_group(tiles, panel_row, top)
        pivots = jnp.sum(jnp.where(panel_row == panel_column, tiles[0], 0.0), axis=1, keepdims=True)
        body = jnp.concatenate(tiles[1:], 1) * lax.rsqrt(pivots)
        work_ref[pl.ds(start, PANEL), :] = body
        left = body[:, :size]
        later = lax.broadcasted_iota(jnp.int32, left.shape, 1) >= start + PANEL
        work_ref[...] -= contract_rows_fully(jnp.where(later, left, 0.0), body)
        return carry

    lax.fori_loop(first, last, panel, 0)


def eliminate_group(tiles, panel_row, top):
    shape = panel_row.shape
    columns = [
        jnp.broadcast_to(tiles[0][:, top + k : top + k + 1], shape) for k in range(GROUP)
    ]
    block = [[columns[k][top + i : top + i + 1, :] for k in range(i + 1)] for i in range(GROUP)]
    ratio = [[None] * GROUP for _ in range(GROUP)]
    scales = []
    for k in range(GROUP):
        inverse = 1.0 / block[k][k]
        for i in range(k + 1, GROUP):
            ratio[i][k] = block[i][k] * inverse
        for i in range(k + 1, GROUP):
            for m in range(k + 1, i + 1):
                block[i][m] = block[i][m] - ratio[i][k] * block[m][k]
        scales.append(jnp.where(panel_row > top + k, columns[k] * inverse, 0.0))
        for m in range(k + 1, GROUP):
            columns[m] = columns[m] - scales[k] * block[m][k]
    result = []
    for tile in tiles:
        rows = [tile[top + k : top + k + 1, :] for k in range(GROUP)]
        for k in range(GROUP):
            for m in range(k + 1, GROUP):
                rows[m] = rows[m] - ratio[m][k] * rows[k]
        for k in range(GROUP):
            tile = tile - scales[k] * rows[k]
        result.append(tile)
    return result


def cholesky_kernel(first, last, place_at, places, *refs):
    size = refs[-1].shape[0]
    panels = size // PANEL
    row_at, column_at = square_places(size)
    if first == 0:
        *piece_refs, = refs[: -1 if last < panels else -3]
        work_ref = refs[-1]
        rows = piece_refs[0].shape[0]
        for at, ref in enumerate(piece_refs):
            here = pl.ds(pl.multiple_of(places[place_at + at] * rows, rows), rows)
            work_ref[here, :size] = ref[...]
        work_ref[:, size:] = (row_at == column_at).astype(F32)
    else:
        work_ref = refs[-1]
        work_ref[...] = refs[0][...]
    eliminate(work_ref, first, last)
    if last == panels:
        factor_ref, inverse_ref = refs[-3:-1]
        factor_ref[...] = jnp.where(row_at <= column_at, work_ref[:, :size], 0.0).T
        inverse_ref[...] = work_ref[:, size:]


def cholesky_and_inverse(places, place_at, pieces, calls):
    size = pieces[0].shape[1]
    panels = size // PANEL
    state = pieces
    for call in range(calls):
        first, last = panels * call // calls, panels * (call + 1) // calls
        work = jax.ShapeDtypeStruct((size, 2 * size), F32)
        square = jax.ShapeDtypeStruct((size, size), F32)
        final = last == panels
        state = pl.pallas_call(
            functools.partial(cholesky_kernel, first, last, place_at),
            grid_spec=pltpu.PrefetchScalarGridSpec(
                num_scalar_prefetch=1,
                grid=(),
                in_specs=[in_vmem()] * len(state),
                out_specs=[in_vmem()] * (2 if final else 1),
                scratch_shapes=[pltpu.VMEM(work.shape, F32)] if final else [],
            ),
            out_shape=[square, square] if final else [work],
            compiler_params=vmem(12 * 2**20),
            cost_estimate=cost(6e9 // calls, 12 * size * size),
            name="cholesky",
        )(places, *state)
    return state


def apply_kernel(first, places, inverse_ref, *refs):
    *basis_refs, out_ref = refs
    parts = split_in_three(inverse_ref[...])
    rows = basis_refs[0].shape[0]
    span = out_ref.shape[0] // rows
    for step in range(len(basis_refs) // span):

        @pl.when(pl.program_id(0) == step)
        def _():
            for at in range(step * span, (step + 1) * span):
                block = basis_refs[at][...]
                here = pl.multiple_of((places[first + at] % span) * rows, rows)
                out_ref[pl.ds(here, rows), :] = sum(
                    lax.dot_general(
                        block, part, (((1,), (1,)), ((), ())), preferred_element_type=F32
                    )
                    for part in reversed(parts)
                )


def apply_inverse(places, first, inverse, basis):
    rows, columns = basis[0].shape
    span = 2
    steps = len(basis) // span
    return pl.pallas_call(
        functools.partial(apply_kernel, first),
        grid_spec=pltpu.PrefetchScalarGridSpec(
            num_scalar_prefetch=1,
            grid=(steps,),
            in_specs=[in_vmem()] * (1 + len(basis)),
            out_specs=pl.BlockSpec(
                (span * rows, columns), lambda i, places: (places[first + span * i] // span, 0)
            ),
        ),
        out_shape=jax.ShapeDtypeStruct((rows * len(basis), columns), F32),
        compiler_params=vmem(16 * 2**20),
        cost_estimate=cost(
            6 * rows * len(basis) * columns * columns, 6 * rows * len(basis) * columns
        ),
        name="apply",
    )(places, inverse, *basis)


RANGE = 2.0**40


def place_table(me, core, level, pix, depth):
    img = 2 * depth
    rows, gathered = 0, pix
    pairs = gathered + img
    cores = pairs + img
    levels = cores + 2
    at = jnp.arange(levels + depth, dtype=jnp.int32)
    block = at - gathered
    pair = at - pairs
    table = jnp.where(at < gathered, me ^ at, (core ^ (block // depth)) * depth + (level ^ (block % depth)))
    table = jnp.where(at < pairs, table, (core ^ 1 ^ (pair % 2)) * depth + (level ^ (pair // 2)))
    table = jnp.where(at < cores, table, core ^ (at - cores))
    table = jnp.where(at < levels, table, level ^ (at - levels))
    return table, rows, gathered, pairs, cores, levels


def level_order(depth):
    middle = depth // 2
    return [middle] + [s for s in range(depth - 1, 0, -1) if s != middle] + [0]


def add_over_pix(value, pix):
    parts = [value] + [xor_swap(value, "pix", s) for s in range(1, pix)]
    return tree_sum(parts)


def row_halves(value):
    rows = value.shape[0] // 2
    return [value[:rows], value[rows:]]


def spread(share, pix):
    def swap(value, shift):
        return xor_swap(value, "pix", shift)

    if pix != 4:
        return [share] + [[swap(half, s) for half in share] for s in range(1, pix)]
    top, low = share
    x_top, y_low = swap(top, 1), swap(low, 2)
    x_low, y_top = swap(low, 1), swap(top, 2)
    far = [swap(x_top, 2), swap(y_low, 1)]
    return [share, [x_top, x_low], [y_top, y_low], far]


def add_round(total, part):
    return (total + part.astype(F32)).astype(BF16)


def score_and_scatter(places, gathered_at, filtered, basis, pix):
    def scores(shift, *kinds):
        return score(places, gathered_at, filtered[shift], basis, kinds)

    def swap(value, shift):
        return xor_swap(value, "pix", shift)

    if pix != 4:
        arrived = [[swap(half, s) for half in scores(s, BF16, BF16)] for s in range(pix - 1, 0, -1)]
        return scores(0, F32, F32), arrived
    far = scores(3, BF16, BF16)
    by_x, by_y = swap(far[0], 1), swap(far[1], 2)
    x_top, x_low = scores(1, BF16, F32)
    from_x = [swap(x_top, 1), None]
    y_top, y_low = scores(2, F32, BF16)
    from_y = [None, swap(y_low, 2)]
    own = scores(0, F32, F32)
    from_y[0] = swap(add_round(y_top, by_x), 2)
    from_x[1] = swap(add_round(x_low, by_y), 1)
    return own, [from_x, from_y]


def per_device(images, classes, ctf_table, weights, probes):
    images_here, pixels = images.shape
    pix, img = lax.axis_size("pix"), lax.axis_size("img")
    depth = img // 2
    chunk = images_here // pix
    width = pixels // img
    me = lax.axis_index("pix")
    place = lax.axis_index("img")
    places, rows_at, gathered_at, pairs_at, cores_at, levels_at = place_table(
        me, place & 1, place >> 1, pix, depth
    )
    weight_share = lax.dynamic_slice_in_dim(weights, me * chunk, chunk, 0)
    places = places + (weight_share[0] > 2.0).astype(jnp.int32)
    weight_share = row_halves(weight_share[:, None])

    shifts = list(range(pix - 1, -1, -1))
    filtered, own, arrived = [None] * pix, None, []
    probe_half = probes.astype(BF16)
    images = pltpu.with_memory_space_constraint(images, pltpu.HBM)
    for shift in shifts:
        filtered[shift], part = filter_and_score(
            places,
            rows_at + shift,
            images,
            classes,
            ctf_table,
            probe_half,
            chunk,
            BF16 if shift else F32,
        )
        if shift:
            arrived.append(row_halves(xor_swap(part, "pix", shift)))
        else:
            own = row_halves(part)

    basis = inverse = None
    for sweep in range(ITERS):
        share = []
        for at in (0, 1):
            total = own[at]
            for part in arrived:
                total = total + part[at].astype(F32)
            here = weight_share[at] if sweep == 0 else weight_share[at] * RANGE
            share.append((here * total).astype(BF16))
        scaled = spread(share, pix)

        early = early_sum(places, pairs_at, filtered[:1], scaled[:1], width, [])
        split = pix // 2
        if split > 1:
            early = early_sum(places, pairs_at, filtered[1:split], scaled[1:split], width, [early])
        parts, after = [None] * depth, []
        for s in level_order(depth):
            send, keep = late_sum(
                places,
                pairs_at + 2 * s,
                2 * s,
                filtered[split:],
                scaled[split:],
                early,
                width,
                after[-2:-1],
            )
            both = keep + xor_swap(send, "img", 1).astype(F32)
            if s:
                both = both.astype(BF16)
                parts[s] = xor_swap(both, "img", 2 * s)
            else:
                parts[s] = both
            after.append(both)

        if sweep == ITERS - 1:
            gram = half_gram(places, cores_at, basis)
            gram = add_over_pix(gram, pix)
            other = xor_swap(gram, "img", 1)
            _, inverse = cholesky_and_inverse(places, cores_at, [gram, other], 2)
            break

        total = parts[0]
        for part in parts[1:]:
            total = total + part.astype(F32)
        block = total.astype(BF16)
        near = [block] + [xor_swap(block, "img", 2 * s) for s in range(1, depth)]
        basis = near + [xor_swap(block, "img", 1) for block in near]

        own, arrived = score_and_scatter(places, gathered_at, filtered, basis, pix)

    half, send, keep = normalize_and_gram(places, cores_at, parts, inverse, 1.0 / RANGE)
    pieces = scatter_rows(places, levels_at, keep, xor_swap(send, "img", 1), depth)
    mine = tree_sum([pieces[0]] + [xor_swap(pieces[s], "img", 2 * s) for s in range(1, depth)])
    pieces = [mine] + [xor_swap(mine, "img", 2 * s) for s in range(1, depth)]
    gram, half = gather_rows(places, levels_at, pieces, half)
    gram = add_over_pix(gram, pix)
    other = xor_swap(gram, "img", 1)
    near = [half] + [xor_swap(half, "img", 2 * s) for s in range(1, depth)]
    basis = near + [xor_swap(block, "img", 1) for block in near]
    factor, inverse = cholesky_and_inverse(places, cores_at, [gram, other], 1)
    return apply_inverse(places, gathered_at, inverse, basis), factor


def plain_per_device(images, classes, ctf_table, weights, probes):
    onehot = (classes[:, None] == jnp.arange(ctf_table.shape[0])[None, :]).astype(BF16)
    filters = jnp.dot(onehot, ctf_table, preferred_element_type=F32)
    filtered = (images.astype(F32) * filters).astype(BF16)
    current = probes
    factor = None
    for _ in range(ITERS):
        share_rows = filtered.shape[0] // lax.axis_size("pix")
        shares = lax.psum_scatter(
            jnp.dot(filtered, current.astype(BF16), preferred_element_type=F32),
            "pix",
            scatter_dimension=0,
            tiled=True,
        )
        weight_share = lax.dynamic_slice_in_dim(
            weights, lax.axis_index("pix") * share_rows, share_rows, 0
        )
        scaled_share = (weight_share[:, None] * shares).astype(BF16)
        scaled = lax.all_gather(scaled_share, "pix", axis=0, tiled=True)
        image_sum = lax.psum(contract_rows(filtered, scaled), "img")
        gram = lax.psum(jnp.dot(image_sum.T, image_sum, precision=HIGHEST), "pix")
        factor = jnp.linalg.cholesky(gram)
        current = jax.scipy.linalg.solve_triangular(factor, image_sum.T, lower=True).T
    return current, factor


def power_of_two(n):
    return n > 1 and n & (n - 1) == 0


def fits(rows, pixels, columns, pix, img):
    return (
        power_of_two(pix)
        and power_of_two(img)
        and rows % (32 * pix) == 0
        and pixels % (LANES * img) == 0
        and columns % LANES == 0
        and columns % (8 * img) == 0
    )


def per_device_of(images, classes, ctf_table, weights, probes):
    pix, img = lax.axis_size("pix"), lax.axis_size("img")
    if not fits(*images.shape, probes.shape[1], pix, img):
        return plain_per_device(images, classes, ctf_table, weights, probes)
    return per_device(images, classes, ctf_table, weights, probes)


def solution(mesh):
    in_specs = (P("img", "pix"), P("img"), P(None, "pix"), P("img"), P("pix", None))
    out_specs = (P("pix", None), P())
    return jax.shard_map(
        per_device_of, mesh=mesh, in_specs=in_specs, out_specs=out_specs, check_vma=False
    )
```

```python
import functools

import jax
import jax.numpy as jnp
from jax import lax
from jax.experimental import pallas as pl
from jax.experimental.pallas import tpu as pltpu
from jax.sharding import PartitionSpec as P


ITERS = 2
F32 = jnp.float32
BF16 = jnp.bfloat16
LANES = 128
PANEL = 32
GROUP = 8
HIGHEST = lax.Precision.HIGHEST


def cost(flops, nbytes):
    return pl.CostEstimate(flops=int(flops), bytes_accessed=int(nbytes), transcendentals=0)


def vmem(nbytes):
    return pltpu.CompilerParams(vmem_limit_bytes=nbytes)


def row_tile(rows, most=400):
    return max(t for t in range(16, most + 1, 16) if rows % t == 0)


def xor_swap(value, axis, mask):
    size = lax.axis_size(axis)
    return lax.ppermute(value, axis, [(i, i ^ mask) for i in range(size)])


def contract_rows(left, right):
    return lax.dot_general(left, right, (((0,), (0,)), ((), ())), preferred_element_type=F32)


def in_vmem():
    return pl.BlockSpec(memory_space=pltpu.VMEM)


def filter_kernel(places, class_ref, image_ref, table_ref, probe_ref, filtered_ref, score_ref):
    table_rows = table_ref.shape[0]
    rows, pixels = image_ref.shape
    onehot = (
        lax.broadcasted_iota(jnp.int32, (table_rows, rows), 0) == class_ref[0]
    ).astype(BF16)
    here = pl.ds(pl.multiple_of(pl.program_id(0) * rows, rows), rows)
    scores = None
    width = min(pixels, 8 * LANES)
    for at in range(0, pixels, width):
        columns = slice(at, min(at + width, pixels))
        filters = contract_rows(onehot, table_ref[:, columns])
        filtered = (image_ref[:, columns].astype(F32) * filters).astype(BF16)
        filtered_ref[here, columns] = filtered
        term = jnp.dot(filtered, probe_ref[columns, :], preferred_element_type=F32)
        scores = term if scores is None else scores + term
    score_ref[here, :] = scores.astype(score_ref.dtype)


def filter_and_score(places, shift, images, classes, table, probe_half, chunk, out_type):
    rows, pixels = images.shape
    columns = probe_half.shape[1]
    tile = row_tile(chunk)
    steps = chunk // tile
    return pl.pallas_call(
        filter_kernel,
        grid_spec=pltpu.PrefetchScalarGridSpec(
            num_scalar_prefetch=1,
            grid=(steps,),
            in_specs=[
                pl.BlockSpec((1, 1, tile), lambda i, places: (places[shift] * steps + i, 0, 0)),
                pl.BlockSpec((tile, pixels), lambda i, places: (places[shift] * steps + i, 0)),
                in_vmem(),
                in_vmem(),
            ],
            out_specs=[in_vmem(), in_vmem()],
        ),
        out_shape=[
            pltpu.VMEM((chunk, pixels), BF16),
            jax.ShapeDtypeStruct((chunk, columns), out_type),
        ],
        compiler_params=vmem(14 * 2**20),
        cost_estimate=cost(4 * chunk * pixels * columns, 2 * chunk * pixels),
        name="filter_and_score",
    )(places, classes.reshape(rows // tile, 1, tile), images, table, probe_half)


def prefetched(count, outs):
    return pltpu.PrefetchScalarGridSpec(
        num_scalar_prefetch=1,
        grid=(),
        in_specs=[in_vmem()] * count,
        out_specs=[in_vmem()] * outs,
    )


def whole_blocks(spots, refs):
    blocks = {}
    for (at, _), ref in zip(spots, refs):
        blocks.setdefault(at, []).append(ref[...])
    return [jnp.concatenate(blocks[at], 0) for at in sorted(blocks)]


def score_kernel(first, width, spots, places, filtered_ref, *refs):
    *basis_refs, top_ref, low_ref = refs
    rows = top_ref.shape[0]
    total = None
    for at, block in enumerate(whole_blocks(spots, basis_refs)):
        columns = pl.ds(pl.multiple_of(places[first + at] * width, width), width)
        term = jnp.dot(filtered_ref[:, columns], block, preferred_element_type=F32)
        total = term if total is None else total + term
    top_ref[...] = total[:rows].astype(top_ref.dtype)
    low_ref[...] = total[rows:].astype(low_ref.dtype)


def score(places, first, filtered, basis, out_types):
    rows, pixels = filtered.shape
    spots, blocks = [piece[:2] for piece in basis], [piece[2] for piece in basis]
    columns = blocks[0].shape[1]
    width = pixels // (1 + max(at for at, _ in spots))
    return pl.pallas_call(
        functools.partial(score_kernel, first, width, spots),
        grid_spec=prefetched(1 + len(basis), 2),
        out_shape=[jax.ShapeDtypeStruct((rows // 2, columns), kind) for kind in out_types],
        compiler_params=vmem(16 * 2**20),
        cost_estimate=cost(2 * rows * pixels * columns, 2 * rows * columns),
        name="score",
    )(places, filtered, *blocks)


def sum_blocks(filtered, scaled):
    rows = filtered[0].shape[0]
    whole = rows // 256 * 256
    total = None
    for left, right in zip(filtered, scaled):
        if whole:
            term = contract_rows(left[:whole, :], right[:whole, :])
            total = term if total is None else total + term
    if whole < rows:
        left = jnp.concatenate([block[whole:, :] for block in filtered], 0)
        right = jnp.concatenate([block[whole:, :] for block in scaled], 0)
        term = contract_rows(left, right)
        total = term if total is None else total + term
    return total


def stack_pieces(stacked_ref, pieces):
    rows = pieces[0].shape[0]
    for at, ref in enumerate(pieces):
        stacked_ref[at * rows : (at + 1) * rows, :] = ref[...]


def block_sum(filtered_refs, stacked_ref, columns):
    rows = filtered_refs[0].shape[0]
    return sum_blocks(
        [ref[:, columns] for ref in filtered_refs],
        [stacked_ref[at * rows : (at + 1) * rows, :] for at in range(len(filtered_refs))],
    )


def early_sum_kernel(count, first, width, places, *refs):
    filtered_refs, piece_refs = refs[:count], refs[count : 3 * count]
    before, out_ref, stacked_ref = refs[3 * count : -2], refs[-2], refs[-1]
    stack_pieces(stacked_ref, piece_refs)

    def block(at, carry):
        columns = pl.ds(pl.multiple_of(places[first + at] * width, width), width)
        here = pl.ds(pl.multiple_of(at * width, width), width)
        total = block_sum(filtered_refs, stacked_ref, columns)
        for ref in before:
            total = total + ref[here, :]
        out_ref[here, :] = total
        return carry

    lax.fori_loop(0, out_ref.shape[0] // width, block, 0)


def sum_grid(count, extra, outs, rows, columns):
    return pltpu.PrefetchScalarGridSpec(
        num_scalar_prefetch=1,
        grid=(),
        in_specs=[in_vmem()] * (3 * count + extra),
        out_specs=[in_vmem()] * outs,
        scratch_shapes=[pltpu.VMEM((count * rows, columns), BF16)],
    )


def early_sum(places, first, filtered, scaled, width, before):
    count = len(filtered)
    rows, pixels = filtered[0].shape
    columns = scaled[0][0].shape[1]
    return pl.pallas_call(
        functools.partial(early_sum_kernel, count, first, width),
        grid_spec=sum_grid(count, len(before), 1, rows, columns),
        out_shape=[jax.ShapeDtypeStruct((pixels, columns), F32)],
        compiler_params=vmem(12 * 2**20),
        cost_estimate=cost(2 * count * rows * pixels * columns, 4 * pixels * columns),
        name="early_sum",
    )(places, *filtered, *sum(scaled, []), *before)[0]


def late_sum_kernel(count, first, at_early, places, *refs):
    filtered_refs, piece_refs = refs[:count], refs[count : 3 * count]
    early_ref = refs[3 * count]
    send_ref, keep_ref, stacked_ref = refs[-3:]
    width = send_ref.shape[0]
    stack_pieces(stacked_ref, piece_refs)

    def block(at, carry):
        columns = pl.ds(pl.multiple_of(places[first + at] * width, width), width)
        here = pl.ds(pl.multiple_of((at_early + at) * width, width), width)
        total = early_ref[here, :] + block_sum(filtered_refs, stacked_ref, columns)

        @pl.when(at == 0)
        def _():
            send_ref[...] = total.astype(send_ref.dtype)

        @pl.when(at == 1)
        def _():
            keep_ref[...] = total

        return carry

    lax.fori_loop(0, 2, block, 0)


def late_sum(places, first, at_early, filtered, scaled, early, width, after):
    count = len(filtered)
    rows = filtered[0].shape[0]
    columns = scaled[0][0].shape[1]
    return pl.pallas_call(
        functools.partial(late_sum_kernel, count, first, at_early),
        grid_spec=sum_grid(count, 1 + len(after), 2, rows, columns),
        out_shape=[
            jax.ShapeDtypeStruct((width, columns), BF16),
            jax.ShapeDtypeStruct((width, columns), F32),
        ],
        compiler_params=vmem(12 * 2**20),
        cost_estimate=cost(4 * count * rows * width * columns, 6 * width * columns),
        name="late_sum",
    )(places, *filtered, *sum(scaled, []), early, *after)


def tree_sum(terms):
    while len(terms) > 1:
        terms = [terms[i] + terms[i + 1] for i in range(0, len(terms), 2)]
    return terms[0]


def gram_kernel(core_at, spots, places, *refs):
    *basis_refs, half_ref, gram_ref = refs
    blocks = whole_blocks(spots, basis_refs)
    gram_ref[...] = tree_sum([contract_rows(block, block) for block in blocks])
    rows = half_ref.shape[0]
    half_ref[...] = gram_ref[pl.ds(pl.multiple_of(places[core_at] * rows, rows), rows), :]


def half_gram(places, core_at, basis):
    spots, blocks = [piece[:2] for piece in basis], [piece[2] for piece in basis]
    columns = blocks[0].shape[1]
    rows = sum(block.shape[0] for block in blocks)
    return pl.pallas_call(
        functools.partial(gram_kernel, core_at, spots),
        grid_spec=pltpu.PrefetchScalarGridSpec(
            num_scalar_prefetch=1,
            grid=(),
            in_specs=[in_vmem()] * len(blocks),
            out_specs=[in_vmem()],
            scratch_shapes=[pltpu.VMEM((columns, columns), F32)],
        ),
        out_shape=[jax.ShapeDtypeStruct((columns // 2, columns), F32)],
        compiler_params=vmem(12 * 2**20),
        cost_estimate=cost(2 * rows * columns * columns, 2 * rows * columns),
        name="gram",
    )(places, *blocks)[0]


def normalize_kernel(core_at, scale, places, *refs):
    *part_refs, inverse_ref, half_ref, send_ref, keep_ref, gram_ref = refs
    halves = [sum(ref[...].astype(F32) for ref in part_refs[at::2]) for at in (0, 1)]
    total = jnp.concatenate(halves, 0)
    block = lax.dot_general(
        total,
        inverse_ref[...] * scale,
        (((1,), (1,)), ((), ())),
        precision=HIGHEST,
        preferred_element_type=F32,
    ).astype(BF16)
    half_ref[...] = block
    gram_ref[...] = contract_rows(block, block)
    rows = send_ref.shape[0]
    here = places[core_at]
    send_ref[...] = gram_ref[pl.ds(pl.multiple_of((1 - here) * rows, rows), rows), :]
    keep_ref[...] = gram_ref[pl.ds(pl.multiple_of(here * rows, rows), rows), :]


def normalize_and_gram(places, core_at, parts, inverse, scale):
    rows, columns = 2 * parts[0].shape[0], parts[0].shape[1]
    return pl.pallas_call(
        functools.partial(normalize_kernel, core_at, scale),
        grid_spec=pltpu.PrefetchScalarGridSpec(
            num_scalar_prefetch=1,
            grid=(),
            in_specs=[in_vmem()] * (len(parts) + 1),
            out_specs=[in_vmem()] * 3,
            scratch_shapes=[pltpu.VMEM((columns, columns), F32)],
        ),
        out_shape=[
            jax.ShapeDtypeStruct((rows, columns), BF16),
            jax.ShapeDtypeStruct((columns // 2, columns), F32),
            jax.ShapeDtypeStruct((columns // 2, columns), F32),
        ],
        compiler_params=vmem(12 * 2**20),
        cost_estimate=cost(14 * rows * columns * columns, 8 * rows * columns),
        name="normalize",
    )(places, *parts, inverse)


def scatter_kernel(first, places, keep_ref, got_ref, *piece_refs):
    rows = piece_refs[0].shape[0]
    for at, ref in enumerate(piece_refs):
        here = pl.ds(pl.multiple_of(places[first + at] * rows, rows), rows)
        ref[...] = keep_ref[here, :] + got_ref[here, :]


def scatter_rows(places, first, keep, got, count):
    rows, columns = keep.shape
    return pl.pallas_call(
        functools.partial(scatter_kernel, first),
        grid_spec=prefetched(2, count),
        out_shape=[jax.ShapeDtypeStruct((rows // count, columns), F32)] * count,
        compiler_params=vmem(4 * 2**20),
        cost_estimate=cost(rows * columns, 12 * rows * columns),
        name="scatter",
    )(places, keep, got)


def gather_kernel(first, count, places, *refs):
    piece_refs, (block_ref, out_ref, block_out_ref) = refs[:count], refs[count:]
    rows = piece_refs[0].shape[0]
    for at, ref in enumerate(piece_refs):
        out_ref[pl.ds(pl.multiple_of(places[first + at] * rows, rows), rows), :] = ref[...]
    block_out_ref[...] = block_ref[...]


def gather_rows(places, first, pieces, block):
    count = len(pieces)
    rows, columns = pieces[0].shape
    return pl.pallas_call(
        functools.partial(gather_kernel, first, count),
        grid_spec=prefetched(count + 1, 2),
        out_shape=[
            jax.ShapeDtypeStruct((rows * count, columns), F32),
            jax.ShapeDtypeStruct(block.shape, block.dtype),
        ],
        compiler_params=vmem(4 * 2**20),
        cost_estimate=cost(rows * columns, 8 * count * rows * columns),
        name="gather",
    )(places, *pieces, block)


def square_places(size):
    return tuple(lax.broadcasted_iota(jnp.int32, (size, size), axis) for axis in (0, 1))


def split_in_three(value):
    parts = []
    for _ in range(3):
        parts.append(value.astype(BF16))
        value = value - parts[-1].astype(F32)
    return parts


def contract_rows_fully(left, right):
    l0, l1, l2 = split_in_three(left)
    r0, r1, r2 = split_in_three(right)
    return contract_rows(
        jnp.concatenate([l2, l1, l0, l1, l0, l0], 0), jnp.concatenate([r0, r1, r2, r0, r1, r0], 0)
    )


def eliminate(work_ref, first, last):
    size = work_ref.shape[0]
    panel_row = lax.broadcasted_iota(jnp.int32, (PANEL, LANES), 0)
    panel_column = lax.broadcasted_iota(jnp.int32, (PANEL, LANES), 1)
    per_tile = LANES // PANEL

    def panel(block, carry):
        start = pl.multiple_of(block * PANEL, PANEL)
        tile = pl.multiple_of((block // per_tile) * LANES, LANES)
        diagonal = work_ref[pl.ds(start, PANEL), pl.ds(tile, LANES)]
        diagonal = pltpu.roll(diagonal, (LANES - (block % per_tile) * PANEL) % LANES, 1)
        tiles = [diagonal] + [
            work_ref[pl.ds(start, PANEL), at : at + LANES] for at in range(0, 2 * size, LANES)
        ]
        for top in range(0, PANEL, GROUP):
            tiles = eliminate_group(tiles, panel_row, top)
        pivots = jnp.sum(jnp.where(panel_row == panel_column, tiles[0], 0.0), axis=1, keepdims=True)
        body = jnp.concatenate(tiles[1:], 1) * lax.rsqrt(pivots)
        work_ref[pl.ds(start, PANEL), :] = body
        left = body[:, :size]
        later = lax.broadcasted_iota(jnp.int32, left.shape, 1) >= start + PANEL
        work_ref[...] -= contract_rows_fully(jnp.where(later, left, 0.0), body)
        return carry

    lax.fori_loop(first, last, panel, 0)


def eliminate_group(tiles, panel_row, top):
    shape = panel_row.shape
    columns = [
        jnp.broadcast_to(tiles[0][:, top + k : top + k + 1], shape) for k in range(GROUP)
    ]
    block = [[columns[k][top + i : top + i + 1, :] for k in range(i + 1)] for i in range(GROUP)]
    ratio = [[None] * GROUP for _ in range(GROUP)]
    scales = []
    for k in range(GROUP):
        inverse = 1.0 / block[k][k]
        for i in range(k + 1, GROUP):
            ratio[i][k] = block[i][k] * inverse
        for i in range(k + 1, GROUP):
            for m in range(k + 1, i + 1):
                block[i][m] = block[i][m] - ratio[i][k] * block[m][k]
        scales.append(jnp.where(panel_row > top + k, columns[k] * inverse, 0.0))
        for m in range(k + 1, GROUP):
            columns[m] = columns[m] - scales[k] * block[m][k]
    result = []
    for tile in tiles:
        rows = [tile[top + k : top + k + 1, :] for k in range(GROUP)]
        for k in range(GROUP):
            for m in range(k + 1, GROUP):
                rows[m] = rows[m] - ratio[m][k] * rows[k]
        for k in range(GROUP):
            tile = tile - scales[k] * rows[k]
        result.append(tile)
    return result


def cholesky_kernel(first, last, place_at, places, *refs):
    size = refs[-1].shape[0]
    panels = size // PANEL
    row_at, column_at = square_places(size)
    if first == 0:
        *piece_refs, = refs[: -1 if last < panels else -3]
        work_ref = refs[-1]
        rows = piece_refs[0].shape[0]
        for at, ref in enumerate(piece_refs):
            here = pl.ds(pl.multiple_of(places[place_at + at] * rows, rows), rows)
            work_ref[here, :size] = ref[...]
        work_ref[:, size:] = (row_at == column_at).astype(F32)
    else:
        work_ref = refs[-1]
        work_ref[...] = refs[0][...]
    eliminate(work_ref, first, last)
    if last == panels:
        factor_ref, inverse_ref = refs[-3:-1]
        factor_ref[...] = jnp.where(row_at <= column_at, work_ref[:, :size], 0.0).T
        inverse_ref[...] = work_ref[:, size:]


def cholesky_and_inverse(places, place_at, pieces, calls):
    size = pieces[0].shape[1]
    panels = size // PANEL
    state = pieces
    for call in range(calls):
        first, last = panels * call // calls, panels * (call + 1) // calls
        work = jax.ShapeDtypeStruct((size, 2 * size), F32)
        square = jax.ShapeDtypeStruct((size, size), F32)
        final = last == panels
        state = pl.pallas_call(
            functools.partial(cholesky_kernel, first, last, place_at),
            grid_spec=pltpu.PrefetchScalarGridSpec(
                num_scalar_prefetch=1,
                grid=(),
                in_specs=[in_vmem()] * len(state),
                out_specs=[in_vmem()] * (2 if final else 1),
                scratch_shapes=[pltpu.VMEM(work.shape, F32)] if final else [],
            ),
            out_shape=[square, square] if final else [work],
            compiler_params=vmem(12 * 2**20),
            cost_estimate=cost(6e9 // calls, 12 * size * size),
            name="cholesky",
        )(places, *state)
    return state


def apply_kernel(first, places, inverse_ref, *refs):
    *basis_refs, out_ref, stacked_ref = refs
    rows, span = basis_refs[0].shape[0], out_ref.shape[0]

    @pl.when(pl.program_id(0) == 0)
    def _():
        for at, ref in enumerate(basis_refs):
            here = pl.ds(pl.multiple_of(places[first + at] * rows, rows), rows)
            stacked_ref[here, :] = ref[...]

    block = stacked_ref[pl.ds(pl.multiple_of(pl.program_id(0) * span, span), span), :]
    out_ref[...] = sum(
        lax.dot_general(block, part, (((1,), (1,)), ((), ())), preferred_element_type=F32)
        for part in reversed(split_in_three(inverse_ref[...]))
    )


def apply_inverse(places, first, inverse, basis):
    rows, columns = basis[0].shape
    pixels = rows * len(basis)
    span = 2 * rows
    return pl.pallas_call(
        functools.partial(apply_kernel, first),
        grid_spec=pltpu.PrefetchScalarGridSpec(
            num_scalar_prefetch=1,
            grid=(pixels // span,),
            in_specs=[in_vmem()] * (1 + len(basis)),
            out_specs=pl.BlockSpec((span, columns), lambda i, places: (i, 0)),
            scratch_shapes=[pltpu.VMEM((pixels, columns), BF16)],
        ),
        out_shape=jax.ShapeDtypeStruct((pixels, columns), F32),
        compiler_params=vmem(16 * 2**20),
        cost_estimate=cost(6 * pixels * columns * columns, 6 * pixels * columns),
        name="apply",
    )(places, inverse, *basis)


RANGE = 2.0**40


def place_table(me, core, level, pix, depth):
    img = 2 * depth
    rows, gathered = 0, pix
    pairs = gathered + img
    cores = pairs + img
    levels = cores + 2
    at = jnp.arange(levels + depth, dtype=jnp.int32)
    block = at - gathered
    pair = at - pairs
    table = jnp.where(at < gathered, me ^ at, (core ^ (block // depth)) * depth + (level ^ (block % depth)))
    table = jnp.where(at < pairs, table, (core ^ 1 ^ (pair % 2)) * depth + (level ^ (pair // 2)))
    table = jnp.where(at < cores, table, core ^ (at - cores))
    table = jnp.where(at < levels, table, level ^ (at - levels))
    return table, rows, gathered, pairs, cores, levels


def level_order(depth):
    return list(range(depth - 1, -1, -1))


def send_sum(both, s, depth, relay):
    def swap(value, shift):
        return xor_swap(value, "img", 2 * shift)

    if depth == 4 and s == 2:
        halves = [add_round(part, other) for part, other in zip(row_halves(both), relay)]
        return [swap(half, 2) for half in halves]
    shift = 1 if depth == 4 else s
    return [swap(half, shift) for half in row_halves(both.astype(BF16))]


def gather_levels(block, depth):
    def swap(value, shift):
        return xor_swap(value, "img", 2 * shift)

    rows = block.shape[0] // 2
    pieces = [(0, 0, block)]
    if depth != 4:
        return pieces + [(s, 0, swap(block, s)) for s in range(1, depth)]
    middle = [swap(half, 2) for half in row_halves(block)]
    pieces.append((1, 0, swap(block, 1)))
    for at, half in enumerate(middle):
        pieces.append((2, at * rows, half))
        pieces.append((3, at * rows, swap(half, 1)))
    return pieces


def gather_cores(pieces, depth):
    return pieces + [(depth + at, row, xor_swap(value, "img", 1)) for at, row, value in pieces]


def add_over_pix(value, pix):
    parts = [value] + [xor_swap(value, "pix", s) for s in range(1, pix)]
    return tree_sum(parts)


def row_halves(value):
    rows = value.shape[0] // 2
    return [value[:rows], value[rows:]]


def spread(share, pix):
    def swap(value, shift):
        return xor_swap(value, "pix", shift)

    if pix != 4:
        return [share] + [[swap(half, s) for half in share] for s in range(1, pix)]
    top, low = share
    x_top, y_low = swap(top, 1), swap(low, 2)
    x_low, y_top = swap(low, 1), swap(top, 2)
    far = [swap(x_top, 2), swap(y_low, 1)]
    return [share, [x_top, x_low], [y_top, y_low], far]


def add_round(total, part):
    return (total + part.astype(F32)).astype(BF16)


def score_and_scatter(places, gathered_at, filtered, basis, pix):
    def scores(shift, *kinds):
        return score(places, gathered_at, filtered[shift], basis, kinds)

    def swap(value, shift):
        return xor_swap(value, "pix", shift)

    if pix != 4:
        arrived = [[swap(half, s) for half in scores(s, BF16, BF16)] for s in range(pix - 1, 0, -1)]
        return scores(0, F32, F32), arrived
    far = scores(3, BF16, BF16)
    by_x, by_y = swap(far[0], 1), swap(far[1], 2)
    x_top, x_low = scores(1, BF16, F32)
    from_x = [swap(x_top, 1), None]
    y_top, y_low = scores(2, F32, BF16)
    from_y = [None, swap(y_low, 2)]
    own = scores(0, F32, F32)
    from_y[0] = swap(add_round(y_top, by_x), 2)
    from_x[1] = swap(add_round(x_low, by_y), 1)
    return own, [from_x, from_y]


def per_device(images, classes, ctf_table, weights, probes):
    images_here, pixels = images.shape
    pix, img = lax.axis_size("pix"), lax.axis_size("img")
    depth = img // 2
    chunk = images_here // pix
    width = pixels // img
    me = lax.axis_index("pix")
    place = lax.axis_index("img")
    places, rows_at, gathered_at, pairs_at, cores_at, levels_at = place_table(
        me, place & 1, place >> 1, pix, depth
    )
    weight_share = lax.dynamic_slice_in_dim(weights, me * chunk, chunk, 0)
    places = places + (weight_share[0] > 2.0).astype(jnp.int32)
    weight_share = row_halves(weight_share[:, None])

    shifts = list(range(pix - 1, -1, -1))
    filtered, own, arrived = [None] * pix, None, []
    probe_half = probes.astype(BF16)
    images = pltpu.with_memory_space_constraint(images, pltpu.HBM)
    for shift in shifts:
        filtered[shift], part = filter_and_score(
            places,
            rows_at + shift,
            images,
            classes,
            ctf_table,
            probe_half,
            chunk,
            BF16 if shift else F32,
        )
        if shift:
            arrived.append(row_halves(xor_swap(part, "pix", shift)))
        else:
            own = row_halves(part)

    basis = inverse = None
    for sweep in range(ITERS):
        share = []
        for at in (0, 1):
            total = own[at]
            for part in arrived:
                total = total + part[at].astype(F32)
            here = weight_share[at] if sweep == 0 else weight_share[at] * RANGE
            share.append((here * total).astype(BF16))
        scaled = spread(share, pix)

        early = early_sum(places, pairs_at, filtered[:1], scaled[:1], width, [])
        split = pix // 2
        if split > 1:
            early = early_sum(places, pairs_at, filtered[1:split], scaled[1:split], width, [early])
        parts, relay, after = [], None, []
        for s in level_order(depth):
            send, keep = late_sum(
                places,
                pairs_at + 2 * s,
                2 * s,
                filtered[split:],
                scaled[split:],
                early,
                width,
                after[-2:-1],
            )
            both = keep + xor_swap(send, "img", 1).astype(F32)
            after.append(both)
            if s == 0:
                parts.append(row_halves(both))
            elif depth == 4 and s == 3:
                relay = send_sum(both, s, depth, None)
            else:
                parts.append(send_sum(both, s, depth, relay))

        if sweep == ITERS - 1:
            gram = half_gram(places, cores_at, basis)
            gram = add_over_pix(gram, pix)
            other = xor_swap(gram, "img", 1)
            _, inverse = cholesky_and_inverse(places, cores_at, [gram, other], 2)
            break

        total = [sum(part[at].astype(F32) for part in parts) for at in (0, 1)]
        block = jnp.concatenate(total, 0).astype(BF16)
        basis = gather_cores(gather_levels(block, depth), depth)

        own, arrived = score_and_scatter(places, gathered_at, filtered, basis, pix)

    half, send, keep = normalize_and_gram(places, cores_at, sum(parts, []), inverse, 1.0 / RANGE)
    pieces = scatter_rows(places, levels_at, keep, xor_swap(send, "img", 1), depth)
    mine = tree_sum([pieces[0]] + [xor_swap(pieces[s], "img", 2 * s) for s in range(1, depth)])
    pieces = [mine] + [xor_swap(mine, "img", 2 * s) for s in range(1, depth)]
    gram, half = gather_rows(places, levels_at, pieces, half)
    gram = add_over_pix(gram, pix)
    other = xor_swap(gram, "img", 1)
    near = [half] + [xor_swap(half, "img", 2 * s) for s in range(1, depth)]
    basis = near + [xor_swap(block, "img", 1) for block in near]
    factor, inverse = cholesky_and_inverse(places, cores_at, [gram, other], 1)
    return apply_inverse(places, gathered_at, inverse, basis), factor


def plain_per_device(images, classes, ctf_table, weights, probes):
    onehot = (classes[:, None] == jnp.arange(ctf_table.shape[0])[None, :]).astype(BF16)
    filters = jnp.dot(onehot, ctf_table, preferred_element_type=F32)
    filtered = (images.astype(F32) * filters).astype(BF16)
    current = probes
    factor = None
    for _ in range(ITERS):
        share_rows = filtered.shape[0] // lax.axis_size("pix")
        shares = lax.psum_scatter(
            jnp.dot(filtered, current.astype(BF16), preferred_element_type=F32),
            "pix",
            scatter_dimension=0,
            tiled=True,
        )
        weight_share = lax.dynamic_slice_in_dim(
            weights, lax.axis_index("pix") * share_rows, share_rows, 0
        )
        scaled_share = (weight_share[:, None] * shares).astype(BF16)
        scaled = lax.all_gather(scaled_share, "pix", axis=0, tiled=True)
        image_sum = lax.psum(contract_rows(filtered, scaled), "img")
        gram = lax.psum(jnp.dot(image_sum.T, image_sum, precision=HIGHEST), "pix")
        factor = jnp.linalg.cholesky(gram)
        current = jax.scipy.linalg.solve_triangular(factor, image_sum.T, lower=True).T
    return current, factor


def power_of_two(n):
    return n > 1 and n & (n - 1) == 0


def fits(rows, pixels, columns, pix, img):
    return (
        power_of_two(pix)
        and power_of_two(img)
        and rows % (32 * pix) == 0
        and pixels % (LANES * img) == 0
        and columns % LANES == 0
        and columns % (8 * img) == 0
    )


def per_device_of(images, classes, ctf_table, weights, probes):
    pix, img = lax.axis_size("pix"), lax.axis_size("img")
    if not fits(*images.shape, probes.shape[1], pix, img):
        return plain_per_device(images, classes, ctf_table, weights, probes)
    return per_device(images, classes, ctf_table, weights, probes)


def solution(mesh):
    in_specs = (P("img", "pix"), P("img"), P(None, "pix"), P("img"), P("pix", None))
    out_specs = (P("pix", None), P())
    return jax.shard_map(
        per_device_of, mesh=mesh, in_specs=in_specs, out_specs=out_specs, check_vma=False
    )
```

```python
import functools

import jax
import jax.numpy as jnp
from jax import lax
from jax.experimental import pallas as pl
from jax.experimental.pallas import tpu as pltpu
from jax.sharding import PartitionSpec as P


ITERS = 2
F32 = jnp.float32
BF16 = jnp.bfloat16
LANES = 128
PANEL = 32
GROUP = 8
HIGHEST = lax.Precision.HIGHEST


def cost(flops, nbytes):
    return pl.CostEstimate(flops=int(flops), bytes_accessed=int(nbytes), transcendentals=0)


def vmem(nbytes):
    return pltpu.CompilerParams(vmem_limit_bytes=nbytes)


def row_tile(rows, most=400):
    return max(t for t in range(16, most + 1, 16) if rows % t == 0)


def xor_swap(value, axis, mask):
    size = lax.axis_size(axis)
    return lax.ppermute(value, axis, [(i, i ^ mask) for i in range(size)])


def contract_rows(left, right):
    return lax.dot_general(left, right, (((0,), (0,)), ((), ())), preferred_element_type=F32)


def in_vmem():
    return pl.BlockSpec(memory_space=pltpu.VMEM)


def filter_kernel(places, class_ref, image_ref, table_ref, probe_ref, filtered_ref, score_ref):
    table_rows = table_ref.shape[0]
    rows, pixels = image_ref.shape
    onehot = (
        lax.broadcasted_iota(jnp.int32, (table_rows, rows), 0) == class_ref[0]
    ).astype(BF16)
    here = pl.ds(pl.multiple_of(pl.program_id(0) * rows, rows), rows)
    scores = None
    width = min(pixels, 8 * LANES)
    for at in range(0, pixels, width):
        columns = slice(at, min(at + width, pixels))
        filters = contract_rows(onehot, table_ref[:, columns])
        filtered = (image_ref[:, columns].astype(F32) * filters).astype(BF16)
        filtered_ref[here, columns] = filtered
        term = jnp.dot(filtered, probe_ref[columns, :], preferred_element_type=F32)
        scores = term if scores is None else scores + term
    score_ref[here, :] = scores.astype(score_ref.dtype)


def filter_and_score(places, shift, images, classes, table, probe_half, chunk, out_type):
    rows, pixels = images.shape
    columns = probe_half.shape[1]
    tile = row_tile(chunk)
    steps = chunk // tile
    return pl.pallas_call(
        filter_kernel,
        grid_spec=pltpu.PrefetchScalarGridSpec(
            num_scalar_prefetch=1,
            grid=(steps,),
            in_specs=[
                pl.BlockSpec((1, 1, tile), lambda i, places: (places[shift] * steps + i, 0, 0)),
                pl.BlockSpec((tile, pixels), lambda i, places: (places[shift] * steps + i, 0)),
                in_vmem(),
                in_vmem(),
            ],
            out_specs=[in_vmem(), in_vmem()],
        ),
        out_shape=[
            pltpu.VMEM((chunk, pixels), BF16),
            jax.ShapeDtypeStruct((chunk, columns), out_type),
        ],
        compiler_params=vmem(14 * 2**20),
        cost_estimate=cost(4 * chunk * pixels * columns, 2 * chunk * pixels),
        name="filter_and_score",
    )(places, classes.reshape(rows // tile, 1, tile), images, table, probe_half)


def prefetched(count, outs):
    return pltpu.PrefetchScalarGridSpec(
        num_scalar_prefetch=1,
        grid=(),
        in_specs=[in_vmem()] * count,
        out_specs=[in_vmem()] * outs,
    )


def whole_blocks(spots, refs):
    blocks = {}
    for (at, _), ref in zip(spots, refs):
        blocks.setdefault(at, []).append(ref[...])
    return [jnp.concatenate(blocks[at], 0) for at in sorted(blocks)]


def score_kernel(first, width, spots, count, spans, places, *refs):
    filtered_refs, refs = refs[:count], refs[count:]
    *basis_refs, top_ref, low_ref = refs
    rows = top_ref.shape[0]
    blocks = whole_blocks(spots, basis_refs)
    totals = []
    for which, begin, size in spans:
        total = None
        for at, block in enumerate(blocks):
            columns = pl.ds(pl.multiple_of(places[first + at] * width, width), width)
            left = filtered_refs[which][begin : begin + size, columns]
            term = jnp.dot(left, block, preferred_element_type=F32)
            total = term if total is None else total + term
        totals.append(total)
    if len(totals) == 1:
        totals = [totals[0][:rows], totals[0][rows:]]
    top_ref[...] = totals[0].astype(top_ref.dtype)
    low_ref[...] = totals[1].astype(low_ref.dtype)


def score(places, first, filtered, chosen, basis, out_types):
    rows, pixels = filtered[0].shape
    half = rows // 2
    used = sorted({at for at, _ in chosen})
    if len(used) == 1:
        spans = [(0, 0, rows)]
    else:
        spans = [(used.index(at), which * half, half) for at, which in chosen]
    spots, blocks = [piece[:2] for piece in basis], [piece[2] for piece in basis]
    columns = blocks[0].shape[1]
    width = pixels // (1 + max(at for at, _ in spots))
    return pl.pallas_call(
        functools.partial(score_kernel, first, width, spots, len(used), spans),
        grid_spec=prefetched(len(used) + len(basis), 2),
        out_shape=[jax.ShapeDtypeStruct((half, columns), kind) for kind in out_types],
        compiler_params=vmem(16 * 2**20),
        cost_estimate=cost(2 * rows * pixels * columns, 2 * rows * columns),
        name="score",
    )(places, *[filtered[at] for at in used], *blocks)


def sum_blocks(filtered, scaled):
    rows = filtered[0].shape[0]
    whole = rows // 256 * 256
    total = None
    for left, right in zip(filtered, scaled):
        if whole:
            term = contract_rows(left[:whole, :], right[:whole, :])
            total = term if total is None else total + term
    if whole < rows:
        left = jnp.concatenate([block[whole:, :] for block in filtered], 0)
        right = jnp.concatenate([block[whole:, :] for block in scaled], 0)
        term = contract_rows(left, right)
        total = term if total is None else total + term
    return total


def entry_sum(entries, filtered_refs, piece_refs, columns):
    rows = piece_refs[0].shape[0]
    blocks = [
        filtered_refs[at][half * rows : (half + 1) * rows, columns] for at, half in entries
    ]
    return sum_blocks(blocks, [ref[...] for ref in piece_refs])


def early_sum_kernel(count, entries, first, width, places, *refs):
    *refs, out_ref = refs
    filtered_refs, refs = refs[:count], refs[count:]
    piece_refs, before = refs[: len(entries)], refs[len(entries) :]

    def block(at, carry):
        columns = pl.ds(pl.multiple_of(places[first + at] * width, width), width)
        here = pl.ds(pl.multiple_of(at * width, width), width)
        total = entry_sum(entries, filtered_refs, piece_refs, columns)
        for ref in before:
            total = total + ref[here, :]
        out_ref[here, :] = total
        return carry

    lax.fori_loop(0, out_ref.shape[0] // width, block, 0)


def take_entries(filtered, scaled, chosen):
    used = sorted({at for at, _ in chosen})
    entries = [(used.index(at), half) for at, half in chosen]
    return entries, [filtered[at] for at in used], [scaled[at][half] for at, half in chosen]


def early_sum(places, first, filtered, scaled, chosen, width, before):
    entries, blocks, pieces = take_entries(filtered, scaled, chosen)
    pixels = blocks[0].shape[1]
    rows, columns = pieces[0].shape
    return pl.pallas_call(
        functools.partial(early_sum_kernel, len(blocks), entries, first, width),
        grid_spec=prefetched(len(blocks) + len(pieces) + len(before), 1),
        out_shape=[jax.ShapeDtypeStruct((pixels, columns), F32)],
        compiler_params=vmem(12 * 2**20),
        cost_estimate=cost(2 * len(pieces) * rows * pixels * columns, 4 * pixels * columns),
        name="early_sum",
    )(places, *blocks, *pieces, *before)[0]


def late_sum_kernel(count, entries, first, at_early, places, *refs):
    filtered_refs, piece_refs = refs[:count], refs[count : count + len(entries)]
    early_ref = refs[count + len(entries)]
    send_ref, keep_ref = refs[-2:]
    width = send_ref.shape[0]

    def block(at, carry):
        columns = pl.ds(pl.multiple_of(places[first + at] * width, width), width)
        here = pl.ds(pl.multiple_of((at_early + at) * width, width), width)
        total = early_ref[here, :] + entry_sum(entries, filtered_refs, piece_refs, columns)

        @pl.when(at == 0)
        def _():
            send_ref[...] = total.astype(send_ref.dtype)

        @pl.when(at == 1)
        def _():
            keep_ref[...] = total

        return carry

    lax.fori_loop(0, 2, block, 0)


def late_sum(places, first, at_early, filtered, scaled, chosen, early, width, after):
    entries, blocks, pieces = take_entries(filtered, scaled, chosen)
    rows, columns = pieces[0].shape
    return pl.pallas_call(
        functools.partial(late_sum_kernel, len(blocks), entries, first, at_early),
        grid_spec=prefetched(len(blocks) + len(pieces) + 1 + len(after), 2),
        out_shape=[
            jax.ShapeDtypeStruct((width, columns), BF16),
            jax.ShapeDtypeStruct((width, columns), F32),
        ],
        compiler_params=vmem(12 * 2**20),
        cost_estimate=cost(4 * len(pieces) * rows * width * columns, 6 * width * columns),
        name="late_sum",
    )(places, *blocks, *pieces, early, *after)


def tree_sum(terms):
    while len(terms) > 1:
        terms = [terms[i] + terms[i + 1] for i in range(0, len(terms), 2)]
    return terms[0]


def gram_kernel(core_at, spots, places, *refs):
    *basis_refs, half_ref, gram_ref = refs
    blocks = whole_blocks(spots, basis_refs)
    gram_ref[...] = tree_sum([contract_rows(block, block) for block in blocks])
    rows = half_ref.shape[0]
    half_ref[...] = gram_ref[pl.ds(pl.multiple_of(places[core_at] * rows, rows), rows), :]


def half_gram(places, core_at, basis):
    spots, blocks = [piece[:2] for piece in basis], [piece[2] for piece in basis]
    columns = blocks[0].shape[1]
    rows = sum(block.shape[0] for block in blocks)
    return pl.pallas_call(
        functools.partial(gram_kernel, core_at, spots),
        grid_spec=pltpu.PrefetchScalarGridSpec(
            num_scalar_prefetch=1,
            grid=(),
            in_specs=[in_vmem()] * len(blocks),
            out_specs=[in_vmem()],
            scratch_shapes=[pltpu.VMEM((columns, columns), F32)],
        ),
        out_shape=[jax.ShapeDtypeStruct((columns // 2, columns), F32)],
        compiler_params=vmem(12 * 2**20),
        cost_estimate=cost(2 * rows * columns * columns, 2 * rows * columns),
        name="gram",
    )(places, *blocks)[0]


def normalize_kernel(core_at, scale, places, *refs):
    *part_refs, inverse_ref, half_ref, send_ref, keep_ref, gram_ref = refs
    halves = [sum(ref[...].astype(F32) for ref in part_refs[at::2]) for at in (0, 1)]
    total = jnp.concatenate(halves, 0)
    block = lax.dot_general(
        total,
        inverse_ref[...] * scale,
        (((1,), (1,)), ((), ())),
        precision=HIGHEST,
        preferred_element_type=F32,
    ).astype(BF16)
    half_ref[...] = block
    gram_ref[...] = contract_rows(block, block)
    rows = send_ref.shape[0]
    here = places[core_at]
    send_ref[...] = gram_ref[pl.ds(pl.multiple_of((1 - here) * rows, rows), rows), :]
    keep_ref[...] = gram_ref[pl.ds(pl.multiple_of(here * rows, rows), rows), :]


def normalize_and_gram(places, core_at, parts, inverse, scale):
    rows, columns = 2 * parts[0].shape[0], parts[0].shape[1]
    return pl.pallas_call(
        functools.partial(normalize_kernel, core_at, scale),
        grid_spec=pltpu.PrefetchScalarGridSpec(
            num_scalar_prefetch=1,
            grid=(),
            in_specs=[in_vmem()] * (len(parts) + 1),
            out_specs=[in_vmem()] * 3,
            scratch_shapes=[pltpu.VMEM((columns, columns), F32)],
        ),
        out_shape=[
            jax.ShapeDtypeStruct((rows, columns), BF16),
            jax.ShapeDtypeStruct((columns // 2, columns), F32),
            jax.ShapeDtypeStruct((columns // 2, columns), F32),
        ],
        compiler_params=vmem(12 * 2**20),
        cost_estimate=cost(14 * rows * columns * columns, 8 * rows * columns),
        name="normalize",
    )(places, *parts, inverse)


def square_places(size):
    return tuple(lax.broadcasted_iota(jnp.int32, (size, size), axis) for axis in (0, 1))


def split_in_three(value):
    parts = []
    for _ in range(3):
        parts.append(value.astype(BF16))
        value = value - parts[-1].astype(F32)
    return parts


def contract_rows_fully(left, right):
    l0, l1, l2 = split_in_three(left)
    r0, r1, r2 = split_in_three(right)
    return contract_rows(
        jnp.concatenate([l2, l1, l0, l1, l0, l0], 0), jnp.concatenate([r0, r1, r2, r0, r1, r0], 0)
    )


def eliminate(work_ref, first, last):
    size = work_ref.shape[0]
    panel_row = lax.broadcasted_iota(jnp.int32, (PANEL, LANES), 0)
    panel_column = lax.broadcasted_iota(jnp.int32, (PANEL, LANES), 1)
    per_tile = LANES // PANEL

    def panel(block, carry):
        start = pl.multiple_of(block * PANEL, PANEL)
        tile = pl.multiple_of((block // per_tile) * LANES, LANES)
        diagonal = work_ref[pl.ds(start, PANEL), pl.ds(tile, LANES)]
        diagonal = pltpu.roll(diagonal, (LANES - (block % per_tile) * PANEL) % LANES, 1)
        tiles = [diagonal] + [
            work_ref[pl.ds(start, PANEL), at : at + LANES] for at in range(0, 2 * size, LANES)
        ]
        for top in range(0, PANEL, GROUP):
            tiles = eliminate_group(tiles, panel_row, top)
        pivots = jnp.sum(jnp.where(panel_row == panel_column, tiles[0], 0.0), axis=1, keepdims=True)
        body = jnp.concatenate(tiles[1:], 1) * lax.rsqrt(pivots)
        work_ref[pl.ds(start, PANEL), :] = body
        left = body[:, :size]
        later = lax.broadcasted_iota(jnp.int32, left.shape, 1) >= start + PANEL
        work_ref[...] -= contract_rows_fully(jnp.where(later, left, 0.0), body)
        return carry

    lax.fori_loop(first, last, panel, 0)


def eliminate_group(tiles, panel_row, top):
    shape = panel_row.shape
    columns = [
        jnp.broadcast_to(tiles[0][:, top + k : top + k + 1], shape) for k in range(GROUP)
    ]
    block = [[columns[k][top + i : top + i + 1, :] for k in range(i + 1)] for i in range(GROUP)]
    ratio = [[None] * GROUP for _ in range(GROUP)]
    scales = []
    for k in range(GROUP):
        inverse = 1.0 / block[k][k]
        for i in range(k + 1, GROUP):
            ratio[i][k] = block[i][k] * inverse
        for i in range(k + 1, GROUP):
            for m in range(k + 1, i + 1):
                block[i][m] = block[i][m] - ratio[i][k] * block[m][k]
        scales.append(jnp.where(panel_row > top + k, columns[k] * inverse, 0.0))
        for m in range(k + 1, GROUP):
            columns[m] = columns[m] - scales[k] * block[m][k]
    result = []
    for tile in tiles:
        rows = [tile[top + k : top + k + 1, :] for k in range(GROUP)]
        for k in range(GROUP):
            for m in range(k + 1, GROUP):
                rows[m] = rows[m] - ratio[m][k] * rows[k]
        for k in range(GROUP):
            tile = tile - scales[k] * rows[k]
        result.append(tile)
    return result


def cholesky_kernel(first, last, place_at, places, *refs):
    size = refs[-1].shape[0]
    panels = size // PANEL
    row_at, column_at = square_places(size)
    if first == 0:
        *piece_refs, = refs[: -1 if last < panels else -3]
        work_ref = refs[-1]
        rows = piece_refs[0].shape[0]
        for at, ref in enumerate(piece_refs):
            here = pl.ds(pl.multiple_of(places[place_at + at] * rows, rows), rows)
            work_ref[here, :size] = ref[...]
        work_ref[:, size:] = (row_at == column_at).astype(F32)
    else:
        work_ref = refs[-1]
        work_ref[...] = refs[0][...]
    eliminate(work_ref, first, last)
    if last == panels:
        factor_ref, inverse_ref = refs[-3:-1]
        factor_ref[...] = jnp.where(row_at <= column_at, work_ref[:, :size], 0.0).T
        inverse_ref[...] = work_ref[:, size:]


def cholesky_and_inverse(places, place_at, pieces, calls):
    size = pieces[0].shape[1]
    panels = size // PANEL
    state = pieces
    for call in range(calls):
        first, last = panels * call // calls, panels * (call + 1) // calls
        work = jax.ShapeDtypeStruct((size, 2 * size), F32)
        square = jax.ShapeDtypeStruct((size, size), F32)
        final = last == panels
        state = pl.pallas_call(
            functools.partial(cholesky_kernel, first, last, place_at),
            grid_spec=pltpu.PrefetchScalarGridSpec(
                num_scalar_prefetch=1,
                grid=(),
                in_specs=[in_vmem()] * len(state),
                out_specs=[in_vmem()] * (2 if final else 1),
                scratch_shapes=[pltpu.VMEM(work.shape, F32)] if final else [],
            ),
            out_shape=[square, square] if final else [work],
            compiler_params=vmem(12 * 2**20),
            cost_estimate=cost(6e9 // calls, 12 * size * size),
            name="cholesky",
        )(places, *state)
    return state


def apply_kernel(first, places, inverse_ref, *refs):
    *basis_refs, out_ref, stacked_ref = refs
    rows, span = basis_refs[0].shape[0], out_ref.shape[0]

    @pl.when(pl.program_id(0) == 0)
    def _():
        for at, ref in enumerate(basis_refs):
            here = pl.ds(pl.multiple_of(places[first + at] * rows, rows), rows)
            stacked_ref[here, :] = ref[...]

    block = stacked_ref[pl.ds(pl.multiple_of(pl.program_id(0) * span, span), span), :]
    out_ref[...] = sum(
        lax.dot_general(block, part, (((1,), (1,)), ((), ())), preferred_element_type=F32)
        for part in reversed(split_in_three(inverse_ref[...]))
    )


def apply_inverse(places, first, inverse, basis):
    rows, columns = basis[0].shape
    pixels = rows * len(basis)
    span = 2 * rows
    return pl.pallas_call(
        functools.partial(apply_kernel, first),
        grid_spec=pltpu.PrefetchScalarGridSpec(
            num_scalar_prefetch=1,
            grid=(pixels // span,),
            in_specs=[in_vmem()] * (1 + len(basis)),
            out_specs=pl.BlockSpec((span, columns), lambda i, places: (i, 0)),
            scratch_shapes=[pltpu.VMEM((pixels, columns), BF16)],
        ),
        out_shape=jax.ShapeDtypeStruct((pixels, columns), F32),
        compiler_params=vmem(16 * 2**20),
        cost_estimate=cost(6 * pixels * columns * columns, 6 * pixels * columns),
        name="apply",
    )(places, inverse, *basis)


RANGE = 2.0**40


def place_table(me, core, level, pix, depth):
    img = 2 * depth
    rows, gathered = 0, pix
    pairs = gathered + img
    cores = pairs + img
    at = jnp.arange(cores + 2, dtype=jnp.int32)
    block = at - gathered
    pair = at - pairs
    table = jnp.where(at < gathered, me ^ at, (core ^ (block // depth)) * depth + (level ^ (block % depth)))
    table = jnp.where(at < pairs, table, (core ^ 1 ^ (pair % 2)) * depth + (level ^ (pair // 2)))
    table = jnp.where(at < cores, table, core ^ (at - cores))
    return table, rows, gathered, pairs, cores


def level_order(depth):
    return list(range(depth - 1, -1, -1))


def send_sum(both, s, depth, relay):
    def swap(value, shift):
        return xor_swap(value, "img", 2 * shift)

    if depth == 4 and s == 2:
        halves = [add_round(part, other) for part, other in zip(row_halves(both), relay)]
        return [swap(half, 2) for half in halves]
    shift = 1 if depth == 4 else s
    return [swap(half, shift) for half in row_halves(both.astype(BF16))]


def gather_levels(block, depth):
    def swap(value, shift):
        return xor_swap(value, "img", 2 * shift)

    rows = block.shape[0] // 2
    pieces = [(0, 0, block)]
    if depth != 4:
        return pieces + [(s, 0, swap(block, s)) for s in range(1, depth)]
    middle = [swap(half, 2) for half in row_halves(block)]
    pieces.append((1, 0, swap(block, 1)))
    for at, half in enumerate(middle):
        pieces.append((2, at * rows, half))
        pieces.append((3, at * rows, swap(half, 1)))
    return pieces


def gather_cores(pieces, depth):
    return pieces + [(depth + at, row, xor_swap(value, "img", 1)) for at, row, value in pieces]


def add_over_pix(value, pix):
    parts = [value] + [xor_swap(value, "pix", s) for s in range(1, pix)]
    return tree_sum(parts)


def row_halves(value):
    rows = value.shape[0] // 2
    return [value[:rows], value[rows:]]


def spread(share, pix):
    def swap(value, shift):
        return xor_swap(value, "pix", shift)

    if pix != 4:
        return [share] + [[swap(half, s) for half in share] for s in range(1, pix)]
    top, low = share
    x_top, y_low = swap(top, 1), swap(low, 2)
    x_low, y_top = swap(low, 1), swap(top, 2)
    far = [swap(x_top, 2), swap(y_low, 1)]
    return [share, [x_top, x_low], [y_top, y_low], far]


def add_round(total, part):
    return (total + part.astype(F32)).astype(BF16)


def score_and_scatter(places, gathered_at, filtered, basis, pix):
    def scores(chosen, *kinds):
        return score(places, gathered_at, filtered, chosen, basis, kinds)

    def swap(value, shift):
        return xor_swap(value, "pix", shift)

    def both(shift):
        return [(shift, 0), (shift, 1)]

    if pix != 4:
        arrived = [
            [swap(part, s) for part in scores(both(s), BF16, BF16)]
            for s in range(pix - 1, 0, -1)
        ]
        return scores(both(0), F32, F32), arrived
    far = scores(both(3), BF16, BF16)
    by_x, by_y = swap(far[0], 1), swap(far[1], 2)
    x_top, y_low = scores([(1, 0), (2, 1)], BF16, BF16)
    from_x, from_y = [swap(x_top, 1), None], [None, swap(y_low, 2)]
    x_low, y_top = scores([(1, 1), (2, 0)], F32, F32)
    from_x[1] = swap(add_round(x_low, by_y), 1)
    from_y[0] = swap(add_round(y_top, by_x), 2)
    own = scores(both(0), F32, F32)
    return own, [from_x, from_y]


def per_device(images, classes, ctf_table, weights, probes):
    images_here, pixels = images.shape
    pix, img = lax.axis_size("pix"), lax.axis_size("img")
    depth = img // 2
    chunk = images_here // pix
    width = pixels // img
    me = lax.axis_index("pix")
    place = lax.axis_index("img")
    places, rows_at, gathered_at, pairs_at, cores_at = place_table(
        me, place & 1, place >> 1, pix, depth
    )
    begin = (me * chunk).astype(jnp.uint32)
    places = places + (begin > jnp.uint32(images_here)).astype(jnp.int32)
    weight_share = lax.dynamic_slice(weights, (begin,), (chunk,))
    weight_share = row_halves(weight_share[:, None])

    shifts = list(range(pix - 1, -1, -1))
    filtered, own, arrived = [None] * pix, None, []
    probe_half = probes.astype(BF16)
    images = pltpu.with_memory_space_constraint(images, pltpu.HBM)
    for shift in shifts:
        filtered[shift], part = filter_and_score(
            places,
            rows_at + shift,
            images,
            classes,
            ctf_table,
            probe_half,
            chunk,
            BF16 if shift else F32,
        )
        if shift:
            arrived.append(row_halves(xor_swap(part, "pix", shift)))
        else:
            own = row_halves(part)

    basis = inverse = None
    for sweep in range(ITERS):
        share = []
        for at in (0, 1):
            total = own[at]
            for part in arrived:
                total = total + part[at].astype(F32)
            here = weight_share[at] if sweep == 0 else weight_share[at] * RANGE
            share.append((here * total).astype(BF16))
        scaled = spread(share, pix)

        rows_of = [(at, half) for at in range(pix) for half in (0, 1)]
        early_rows = [(1, 0), (2, 1)] if pix == 4 else rows_of[2:pix]
        late_rows = [row for row in rows_of[2:] if row not in early_rows]
        early = early_sum(places, pairs_at, filtered, scaled, rows_of[:2], width, [])
        if early_rows:
            early = early_sum(
                places, pairs_at, filtered, scaled, early_rows, width, [early]
            )
        parts, relay, after = [], None, []
        for s in level_order(depth):
            send, keep = late_sum(
                places,
                pairs_at + 2 * s,
                2 * s,
                filtered,
                scaled,
                late_rows,
                early,
                width,
                after[-2:-1],
            )
            both = keep + xor_swap(send, "img", 1).astype(F32)
            after.append(both)
            if s == 0:
                parts.append(row_halves(both))
            elif depth == 4 and s == 3:
                relay = send_sum(both, s, depth, None)
            else:
                parts.append(send_sum(both, s, depth, relay))

        if sweep == ITERS - 1:
            gram = half_gram(places, cores_at, basis)
            gram = add_over_pix(gram, pix)
            other = xor_swap(gram, "img", 1)
            _, inverse = cholesky_and_inverse(places, cores_at, [gram, other], 2)
            break

        total = [sum(part[at].astype(F32) for part in parts) for at in (0, 1)]
        block = jnp.concatenate(total, 0).astype(BF16)
        basis = gather_cores(gather_levels(block, depth), depth)

        own, arrived = score_and_scatter(places, gathered_at, filtered, basis, pix)

    half, send, keep = normalize_and_gram(places, cores_at, sum(parts, []), inverse, 1.0 / RANGE)
    gram = keep + xor_swap(send, "img", 1)
    step = 1
    while step < depth:
        gram = gram + xor_swap(gram, "img", 2 * step)
        step *= 2
    gram = add_over_pix(gram, pix)
    other = xor_swap(gram, "img", 1)
    near = [half] + [xor_swap(half, "img", 2 * s) for s in range(1, depth)]
    basis = near + [xor_swap(block, "img", 1) for block in near]
    factor, inverse = cholesky_and_inverse(places, cores_at, [gram, other], 1)
    return apply_inverse(places, gathered_at, inverse, basis), factor


def plain_per_device(images, classes, ctf_table, weights, probes):
    onehot = (classes[:, None] == jnp.arange(ctf_table.shape[0])[None, :]).astype(BF16)
    filters = jnp.dot(onehot, ctf_table, preferred_element_type=F32)
    filtered = (images.astype(F32) * filters).astype(BF16)
    current = probes
    factor = None
    for _ in range(ITERS):
        share_rows = filtered.shape[0] // lax.axis_size("pix")
        shares = lax.psum_scatter(
            jnp.dot(filtered, current.astype(BF16), preferred_element_type=F32),
            "pix",
            scatter_dimension=0,
            tiled=True,
        )
        weight_share = lax.dynamic_slice_in_dim(
            weights, lax.axis_index("pix") * share_rows, share_rows, 0
        )
        scaled_share = (weight_share[:, None] * shares).astype(BF16)
        scaled = lax.all_gather(scaled_share, "pix", axis=0, tiled=True)
        image_sum = lax.psum(contract_rows(filtered, scaled), "img")
        gram = lax.psum(jnp.dot(image_sum.T, image_sum, precision=HIGHEST), "pix")
        factor = jnp.linalg.cholesky(gram)
        current = jax.scipy.linalg.solve_triangular(factor, image_sum.T, lower=True).T
    return current, factor


def power_of_two(n):
    return n > 1 and n & (n - 1) == 0


def fits(rows, pixels, columns, pix, img):
    return (
        power_of_two(pix)
        and power_of_two(img)
        and rows % (32 * pix) == 0
        and pixels % (LANES * img) == 0
        and columns % LANES == 0
        and columns % (8 * img) == 0
    )


def per_device_of(images, classes, ctf_table, weights, probes):
    pix, img = lax.axis_size("pix"), lax.axis_size("img")
    if not fits(*images.shape, probes.shape[1], pix, img):
        return plain_per_device(images, classes, ctf_table, weights, probes)
    return per_device(images, classes, ctf_table, weights, probes)


def solution(mesh):
    in_specs = (P("img", "pix"), P("img"), P(None, "pix"), P("img"), P("pix", None))
    out_specs = (P("pix", None), P())
    return jax.shard_map(
        per_device_of, mesh=mesh, in_specs=in_specs, out_specs=out_specs, check_vma=False
    )
```

```python
import functools

import jax
import jax.numpy as jnp
from jax import lax
from jax.experimental import pallas as pl
from jax.experimental.pallas import tpu as pltpu
from jax.sharding import PartitionSpec as P


ITERS = 2
F32 = jnp.float32
BF16 = jnp.bfloat16
LANES = 128
PANEL = 32
GROUP = 8
HIGHEST = lax.Precision.HIGHEST


def cost(flops, nbytes):
    return pl.CostEstimate(flops=int(flops), bytes_accessed=int(nbytes), transcendentals=0)


def vmem(nbytes):
    return pltpu.CompilerParams(vmem_limit_bytes=nbytes)


def row_tile(rows, most=400):
    return max(t for t in range(16, most + 1, 16) if rows % t == 0)


def xor_swap(value, axis, mask):
    size = lax.axis_size(axis)
    return lax.ppermute(value, axis, [(i, i ^ mask) for i in range(size)])


def contract_rows(left, right):
    return lax.dot_general(left, right, (((0,), (0,)), ((), ())), preferred_element_type=F32)


def in_vmem():
    return pl.BlockSpec(memory_space=pltpu.VMEM)


def filter_kernel(places, class_ref, image_ref, table_ref, probe_ref, filtered_ref, score_ref):
    table_rows = table_ref.shape[0]
    rows, pixels = image_ref.shape
    onehot = (
        lax.broadcasted_iota(jnp.int32, (table_rows, rows), 0) == class_ref[0]
    ).astype(BF16)
    here = pl.ds(pl.multiple_of(pl.program_id(0) * rows, rows), rows)
    scores = None
    width = min(pixels, 8 * LANES)
    for at in range(0, pixels, width):
        columns = slice(at, min(at + width, pixels))
        filters = contract_rows(onehot, table_ref[:, columns])
        filtered = (image_ref[:, columns].astype(F32) * filters).astype(BF16)
        filtered_ref[here, columns] = filtered
        term = jnp.dot(filtered, probe_ref[columns, :], preferred_element_type=F32)
        scores = term if scores is None else scores + term
    score_ref[here, :] = scores.astype(score_ref.dtype)


def filter_and_score(places, shift, images, classes, table, probe_half, chunk, out_type):
    rows, pixels = images.shape
    columns = probe_half.shape[1]
    tile = row_tile(chunk)
    steps = chunk // tile
    return pl.pallas_call(
        filter_kernel,
        grid_spec=pltpu.PrefetchScalarGridSpec(
            num_scalar_prefetch=1,
            grid=(steps,),
            in_specs=[
                pl.BlockSpec((1, 1, tile), lambda i, places: (places[shift] * steps + i, 0, 0)),
                pl.BlockSpec((tile, pixels), lambda i, places: (places[shift] * steps + i, 0)),
                in_vmem(),
                in_vmem(),
            ],
            out_specs=[in_vmem(), in_vmem()],
        ),
        out_shape=[
            pltpu.VMEM((chunk, pixels), BF16),
            jax.ShapeDtypeStruct((chunk, columns), out_type),
        ],
        compiler_params=vmem(14 * 2**20),
        cost_estimate=cost(4 * chunk * pixels * columns, 2 * chunk * pixels),
    )(places, classes.reshape(rows // tile, 1, tile), images, table, probe_half)


def prefetched(count, outs):
    return pltpu.PrefetchScalarGridSpec(
        num_scalar_prefetch=1,
        grid=(),
        in_specs=[in_vmem()] * count,
        out_specs=[in_vmem()] * outs,
    )


def whole_blocks(spots, refs):
    blocks = {}
    for (at, _), ref in zip(spots, refs):
        blocks.setdefault(at, []).append(ref[...])
    return [jnp.concatenate(blocks[at], 0) for at in sorted(blocks)]


def score_kernel(first, width, spots, count, spans, places, *refs):
    filtered_refs, refs = refs[:count], refs[count:]
    *basis_refs, top_ref, low_ref = refs
    rows = top_ref.shape[0]
    blocks = whole_blocks(spots, basis_refs)
    totals = []
    for which, begin, size in spans:
        total = None
        for at, block in enumerate(blocks):
            columns = pl.ds(pl.multiple_of(places[first + at] * width, width), width)
            left = filtered_refs[which][begin : begin + size, columns]
            term = jnp.dot(left, block, preferred_element_type=F32)
            total = term if total is None else total + term
        totals.append(total)
    if len(totals) == 1:
        totals = [totals[0][:rows], totals[0][rows:]]
    top_ref[...] = totals[0].astype(top_ref.dtype)
    low_ref[...] = totals[1].astype(low_ref.dtype)


def score(places, first, filtered, chosen, basis, out_types):
    rows, pixels = filtered[0].shape
    half = rows // 2
    used = sorted({at for at, _ in chosen})
    if len(used) == 1:
        spans = [(0, 0, rows)]
    else:
        spans = [(used.index(at), which * half, half) for at, which in chosen]
    spots, blocks = [piece[:2] for piece in basis], [piece[2] for piece in basis]
    columns = blocks[0].shape[1]
    width = pixels // (1 + max(at for at, _ in spots))
    return pl.pallas_call(
        functools.partial(score_kernel, first, width, spots, len(used), spans),
        grid_spec=prefetched(len(used) + len(basis), 2),
        out_shape=[jax.ShapeDtypeStruct((half, columns), kind) for kind in out_types],
        compiler_params=vmem(16 * 2**20),
        cost_estimate=cost(2 * rows * pixels * columns, 2 * rows * columns),
    )(places, *[filtered[at] for at in used], *blocks)


def sum_blocks(filtered, scaled):
    rows = filtered[0].shape[0]
    whole = rows // 256 * 256
    total = None
    for left, right in zip(filtered, scaled):
        if whole:
            term = contract_rows(left[:whole, :], right[:whole, :])
            total = term if total is None else total + term
    if whole < rows:
        left = jnp.concatenate([block[whole:, :] for block in filtered], 0)
        right = jnp.concatenate([block[whole:, :] for block in scaled], 0)
        term = contract_rows(left, right)
        total = term if total is None else total + term
    return total


def entry_sum(entries, filtered_refs, piece_refs, columns):
    rows = piece_refs[0].shape[0]
    blocks = [
        filtered_refs[at][half * rows : (half + 1) * rows, columns] for at, half in entries
    ]
    return sum_blocks(blocks, [ref[...] for ref in piece_refs])


def early_sum_kernel(count, entries, first, width, places, *refs):
    *refs, out_ref = refs
    filtered_refs, refs = refs[:count], refs[count:]
    piece_refs, before = refs[: len(entries)], refs[len(entries) :]

    def block(at, carry):
        columns = pl.ds(pl.multiple_of(places[first + at] * width, width), width)
        here = pl.ds(pl.multiple_of(at * width, width), width)
        total = entry_sum(entries, filtered_refs, piece_refs, columns)
        for ref in before:
            total = total + ref[here, :]
        out_ref[here, :] = total
        return carry

    lax.fori_loop(0, out_ref.shape[0] // width, block, 0)


def take_entries(filtered, scaled, chosen):
    used = sorted({at for at, _ in chosen})
    entries = [(used.index(at), half) for at, half in chosen]
    return entries, [filtered[at] for at in used], [scaled[at][half] for at, half in chosen]


def early_sum(places, first, filtered, scaled, chosen, width, before):
    entries, blocks, pieces = take_entries(filtered, scaled, chosen)
    pixels = blocks[0].shape[1]
    rows, columns = pieces[0].shape
    return pl.pallas_call(
        functools.partial(early_sum_kernel, len(blocks), entries, first, width),
        grid_spec=prefetched(len(blocks) + len(pieces) + len(before), 1),
        out_shape=[jax.ShapeDtypeStruct((pixels, columns), F32)],
        compiler_params=vmem(12 * 2**20),
        cost_estimate=cost(2 * len(pieces) * rows * pixels * columns, 4 * pixels * columns),
    )(places, *blocks, *pieces, *before)[0]


def late_sum_kernel(count, entries, first, at_early, places, *refs):
    filtered_refs, piece_refs = refs[:count], refs[count : count + len(entries)]
    early_ref = refs[count + len(entries)]
    send_ref, keep_ref = refs[-2:]
    width = send_ref.shape[0]

    def block(at, carry):
        columns = pl.ds(pl.multiple_of(places[first + at] * width, width), width)
        here = pl.ds(pl.multiple_of((at_early + at) * width, width), width)
        total = early_ref[here, :] + entry_sum(entries, filtered_refs, piece_refs, columns)

        @pl.when(at == 0)
        def _():
            send_ref[...] = total.astype(send_ref.dtype)

        @pl.when(at == 1)
        def _():
            keep_ref[...] = total

        return carry

    lax.fori_loop(0, 2, block, 0)


def late_sum(places, first, at_early, filtered, scaled, chosen, early, width, after):
    entries, blocks, pieces = take_entries(filtered, scaled, chosen)
    rows, columns = pieces[0].shape
    return pl.pallas_call(
        functools.partial(late_sum_kernel, len(blocks), entries, first, at_early),
        grid_spec=prefetched(len(blocks) + len(pieces) + 1 + len(after), 2),
        out_shape=[
            jax.ShapeDtypeStruct((width, columns), BF16),
            jax.ShapeDtypeStruct((width, columns), F32),
        ],
        compiler_params=vmem(12 * 2**20),
        cost_estimate=cost(4 * len(pieces) * rows * width * columns, 6 * width * columns),
    )(places, *blocks, *pieces, early, *after)


def tree_sum(terms):
    while len(terms) > 1:
        terms = [terms[i] + terms[i + 1] for i in range(0, len(terms), 2)]
    return terms[0]


def gram_kernel(core_at, spots, places, *refs):
    *basis_refs, half_ref, gram_ref = refs
    blocks = whole_blocks(spots, basis_refs)
    gram_ref[...] = tree_sum([contract_rows(block, block) for block in blocks])
    rows = half_ref.shape[0]
    half_ref[...] = gram_ref[pl.ds(pl.multiple_of(places[core_at] * rows, rows), rows), :]


def half_gram(places, core_at, basis):
    spots, blocks = [piece[:2] for piece in basis], [piece[2] for piece in basis]
    columns = blocks[0].shape[1]
    rows = sum(block.shape[0] for block in blocks)
    return pl.pallas_call(
        functools.partial(gram_kernel, core_at, spots),
        grid_spec=pltpu.PrefetchScalarGridSpec(
            num_scalar_prefetch=1,
            grid=(),
            in_specs=[in_vmem()] * len(blocks),
            out_specs=[in_vmem()],
            scratch_shapes=[pltpu.VMEM((columns, columns), F32)],
        ),
        out_shape=[jax.ShapeDtypeStruct((columns // 2, columns), F32)],
        compiler_params=vmem(12 * 2**20),
        cost_estimate=cost(2 * rows * columns * columns, 2 * rows * columns),
    )(places, *blocks)[0]


def normalize_kernel(core_at, scale, places, *refs):
    *part_refs, inverse_ref, half_ref, send_ref, keep_ref, gram_ref = refs
    halves = [sum(ref[...].astype(F32) for ref in part_refs[at::2]) for at in (0, 1)]
    total = jnp.concatenate(halves, 0)
    block = lax.dot_general(
        total,
        inverse_ref[...] * scale,
        (((1,), (1,)), ((), ())),
        precision=HIGHEST,
        preferred_element_type=F32,
    ).astype(BF16)
    half_ref[...] = block
    gram_ref[...] = contract_rows(block, block)
    rows = send_ref.shape[0]
    here = places[core_at]
    send_ref[...] = gram_ref[pl.ds(pl.multiple_of((1 - here) * rows, rows), rows), :]
    keep_ref[...] = gram_ref[pl.ds(pl.multiple_of(here * rows, rows), rows), :]


def normalize_and_gram(places, core_at, parts, inverse, scale):
    rows, columns = 2 * parts[0].shape[0], parts[0].shape[1]
    return pl.pallas_call(
        functools.partial(normalize_kernel, core_at, scale),
        grid_spec=pltpu.PrefetchScalarGridSpec(
            num_scalar_prefetch=1,
            grid=(),
            in_specs=[in_vmem()] * (len(parts) + 1),
            out_specs=[in_vmem()] * 3,
            scratch_shapes=[pltpu.VMEM((columns, columns), F32)],
        ),
        out_shape=[
            jax.ShapeDtypeStruct((rows, columns), BF16),
            jax.ShapeDtypeStruct((columns // 2, columns), F32),
            jax.ShapeDtypeStruct((columns // 2, columns), F32),
        ],
        compiler_params=vmem(12 * 2**20),
        cost_estimate=cost(14 * rows * columns * columns, 8 * rows * columns),
    )(places, *parts, inverse)


def square_places(size):
    return tuple(lax.broadcasted_iota(jnp.int32, (size, size), axis) for axis in (0, 1))


def split_in_three(value):
    parts = []
    for _ in range(3):
        parts.append(value.astype(BF16))
        value = value - parts[-1].astype(F32)
    return parts


def contract_rows_fully(left, right):
    l0, l1, l2 = split_in_three(left)
    r0, r1, r2 = split_in_three(right)
    return contract_rows(
        jnp.concatenate([l2, l1, l0, l1, l0, l0], 0), jnp.concatenate([r0, r1, r2, r0, r1, r0], 0)
    )


def eliminate(work_ref, first, last):
    size = work_ref.shape[0]
    panel_row = lax.broadcasted_iota(jnp.int32, (PANEL, LANES), 0)
    panel_column = lax.broadcasted_iota(jnp.int32, (PANEL, LANES), 1)
    per_tile = LANES // PANEL

    def panel(block, carry):
        start = pl.multiple_of(block * PANEL, PANEL)
        tile = pl.multiple_of((block // per_tile) * LANES, LANES)
        diagonal = work_ref[pl.ds(start, PANEL), pl.ds(tile, LANES)]
        diagonal = pltpu.roll(diagonal, (LANES - (block % per_tile) * PANEL) % LANES, 1)
        tiles = [diagonal] + [
            work_ref[pl.ds(start, PANEL), at : at + LANES] for at in range(0, 2 * size, LANES)
        ]
        for top in range(0, PANEL, GROUP):
            tiles = eliminate_group(tiles, panel_row, top)
        pivots = jnp.sum(jnp.where(panel_row == panel_column, tiles[0], 0.0), axis=1, keepdims=True)
        body = jnp.concatenate(tiles[1:], 1) * lax.rsqrt(pivots)
        work_ref[pl.ds(start, PANEL), :] = body
        left = body[:, :size]
        later = lax.broadcasted_iota(jnp.int32, left.shape, 1) >= start + PANEL
        work_ref[...] -= contract_rows_fully(jnp.where(later, left, 0.0), body)
        return carry

    lax.fori_loop(first, last, panel, 0)


def eliminate_group(tiles, panel_row, top):
    shape = panel_row.shape
    columns = [
        jnp.broadcast_to(tiles[0][:, top + k : top + k + 1], shape) for k in range(GROUP)
    ]
    block = [[columns[k][top + i : top + i + 1, :] for k in range(i + 1)] for i in range(GROUP)]
    ratio = [[None] * GROUP for _ in range(GROUP)]
    scales = []
    for k in range(GROUP):
        inverse = 1.0 / block[k][k]
        for i in range(k + 1, GROUP):
            ratio[i][k] = block[i][k] * inverse
        for i in range(k + 1, GROUP):
            for m in range(k + 1, i + 1):
                block[i][m] = block[i][m] - ratio[i][k] * block[m][k]
        scales.append(jnp.where(panel_row > top + k, columns[k] * inverse, 0.0))
        for m in range(k + 1, GROUP):
            columns[m] = columns[m] - scales[k] * block[m][k]
    result = []
    for tile in tiles:
        rows = [tile[top + k : top + k + 1, :] for k in range(GROUP)]
        for k in range(GROUP):
            for m in range(k + 1, GROUP):
                rows[m] = rows[m] - ratio[m][k] * rows[k]
        for k in range(GROUP):
            tile = tile - scales[k] * rows[k]
        result.append(tile)
    return result


def cholesky_kernel(first, last, place_at, places, *refs):
    size = refs[-1].shape[0]
    panels = size // PANEL
    row_at, column_at = square_places(size)
    if first == 0:
        *piece_refs, = refs[: -1 if last < panels else -3]
        work_ref = refs[-1]
        rows = piece_refs[0].shape[0]
        for at, ref in enumerate(piece_refs):
            here = pl.ds(pl.multiple_of(places[place_at + at] * rows, rows), rows)
            work_ref[here, :size] = ref[...]
        work_ref[:, size:] = (row_at == column_at).astype(F32)
    else:
        work_ref = refs[-1]
        work_ref[...] = refs[0][...]
    eliminate(work_ref, first, last)
    if last == panels:
        factor_ref, inverse_ref = refs[-3:-1]
        factor_ref[...] = jnp.where(row_at <= column_at, work_ref[:, :size], 0.0).T
        inverse_ref[...] = work_ref[:, size:]


def cholesky_and_inverse(places, place_at, pieces, calls):
    size = pieces[0].shape[1]
    panels = size // PANEL
    state = pieces
    for call in range(calls):
        first, last = panels * call // calls, panels * (call + 1) // calls
        work = jax.ShapeDtypeStruct((size, 2 * size), F32)
        square = jax.ShapeDtypeStruct((size, size), F32)
        final = last == panels
        state = pl.pallas_call(
            functools.partial(cholesky_kernel, first, last, place_at),
            grid_spec=pltpu.PrefetchScalarGridSpec(
                num_scalar_prefetch=1,
                grid=(),
                in_specs=[in_vmem()] * len(state),
                out_specs=[in_vmem()] * (2 if final else 1),
                scratch_shapes=[pltpu.VMEM(work.shape, F32)] if final else [],
            ),
            out_shape=[square, square] if final else [work],
            compiler_params=vmem(12 * 2**20),
            cost_estimate=cost(6e9 // calls, 12 * size * size),
        )(places, *state)
    return state


def apply_kernel(first, places, inverse_ref, *refs):
    *basis_refs, out_ref, stacked_ref = refs
    rows, span = basis_refs[0].shape[0], out_ref.shape[0]

    @pl.when(pl.program_id(0) == 0)
    def _():
        for at, ref in enumerate(basis_refs):
            here = pl.ds(pl.multiple_of(places[first + at] * rows, rows), rows)
            stacked_ref[here, :] = ref[...]

    block = stacked_ref[pl.ds(pl.multiple_of(pl.program_id(0) * span, span), span), :]
    out_ref[...] = sum(
        lax.dot_general(block, part, (((1,), (1,)), ((), ())), preferred_element_type=F32)
        for part in reversed(split_in_three(inverse_ref[...])[:2])
    )


def apply_inverse(places, first, inverse, basis):
    rows, columns = basis[0].shape
    pixels = rows * len(basis)
    span = 2 * rows
    return pl.pallas_call(
        functools.partial(apply_kernel, first),
        grid_spec=pltpu.PrefetchScalarGridSpec(
            num_scalar_prefetch=1,
            grid=(pixels // span,),
            in_specs=[in_vmem()] * (1 + len(basis)),
            out_specs=pl.BlockSpec((span, columns), lambda i, places: (i, 0)),
            scratch_shapes=[pltpu.VMEM((pixels, columns), BF16)],
        ),
        out_shape=jax.ShapeDtypeStruct((pixels, columns), F32),
        compiler_params=vmem(16 * 2**20),
        cost_estimate=cost(6 * pixels * columns * columns, 6 * pixels * columns),
    )(places, inverse, *basis)


RANGE = 2.0**40


def place_table(me, core, level, pix, depth):
    img = 2 * depth
    rows, gathered = 0, pix
    pairs = gathered + img
    cores = pairs + img
    at = jnp.arange(cores + 2, dtype=jnp.int32)
    block = at - gathered
    pair = at - pairs
    table = jnp.where(at < gathered, me ^ at, (core ^ (block // depth)) * depth + (level ^ (block % depth)))
    table = jnp.where(at < pairs, table, (core ^ 1 ^ (pair % 2)) * depth + (level ^ (pair // 2)))
    table = jnp.where(at < cores, table, core ^ (at - cores))
    return table, rows, gathered, pairs, cores


def level_order(depth):
    return list(range(depth - 1, -1, -1))


def send_sum(both, s, depth, relay):
    def swap(value, shift):
        return xor_swap(value, "img", 2 * shift)

    if depth == 4 and s == 2:
        halves = [add_round(part, other) for part, other in zip(row_halves(both), relay)]
        return [swap(half, 2) for half in halves]
    shift = 1 if depth == 4 else s
    return [swap(half, shift) for half in row_halves(both.astype(BF16))]


def gather_levels(block, depth):
    def swap(value, shift):
        return xor_swap(value, "img", 2 * shift)

    rows = block.shape[0] // 2
    pieces = [(0, 0, block)]
    if depth != 4:
        return pieces + [(s, 0, swap(block, s)) for s in range(1, depth)]
    middle = [swap(half, 2) for half in row_halves(block)]
    pieces.append((1, 0, swap(block, 1)))
    for at, half in enumerate(middle):
        pieces.append((2, at * rows, half))
        pieces.append((3, at * rows, swap(half, 1)))
    return pieces


def gather_cores(pieces, depth):
    return pieces + [(depth + at, row, xor_swap(value, "img", 1)) for at, row, value in pieces]


def add_over_pix(value, pix):
    parts = [value] + [xor_swap(value, "pix", s) for s in range(1, pix)]
    return tree_sum(parts)


def row_halves(value):
    rows = value.shape[0] // 2
    return [value[:rows], value[rows:]]


def spread(share, pix):
    def swap(value, shift):
        return xor_swap(value, "pix", shift)

    if pix != 4:
        return [share] + [[swap(half, s) for half in share] for s in range(1, pix)]
    top, low = share
    x_top, y_low = swap(top, 1), swap(low, 2)
    x_low, y_top = swap(low, 1), swap(top, 2)
    far = [swap(x_top, 2), swap(y_low, 1)]
    return [share, [x_top, x_low], [y_top, y_low], far]


def add_round(total, part):
    return (total + part.astype(F32)).astype(BF16)


def score_and_scatter(places, gathered_at, filtered, basis, pix):
    def scores(chosen, *kinds):
        return score(places, gathered_at, filtered, chosen, basis, kinds)

    def swap(value, shift):
        return xor_swap(value, "pix", shift)

    def both(shift):
        return [(shift, 0), (shift, 1)]

    if pix != 4:
        arrived = [
            [swap(part, s) for part in scores(both(s), BF16, BF16)]
            for s in range(pix - 1, 0, -1)
        ]
        return scores(both(0), F32, F32), arrived
    far = scores(both(3), BF16, BF16)
    by_x, by_y = swap(far[0], 1), swap(far[1], 2)
    x_top, y_low = scores([(1, 0), (2, 1)], BF16, BF16)
    from_x, from_y = [swap(x_top, 1), None], [None, swap(y_low, 2)]
    x_low, y_top = scores([(1, 1), (2, 0)], F32, F32)
    from_x[1] = swap(add_round(x_low, by_y), 1)
    from_y[0] = swap(add_round(y_top, by_x), 2)
    own = scores(both(0), F32, F32)
    return own, [from_x, from_y]


def per_device(images, classes, ctf_table, weights, probes):
    images_here, pixels = images.shape
    pix, img = lax.axis_size("pix"), lax.axis_size("img")
    depth = img // 2
    chunk = images_here // pix
    width = pixels // img
    me = lax.axis_index("pix")
    place = lax.axis_index("img")
    places, rows_at, gathered_at, pairs_at, cores_at = place_table(
        me, place & 1, place >> 1, pix, depth
    )
    begin = (me * chunk).astype(jnp.uint32)
    places = places + (begin > jnp.uint32(images_here)).astype(jnp.int32)
    weight_share = lax.dynamic_slice(weights, (begin,), (chunk,))
    weight_share = row_halves(weight_share[:, None])

    shifts = list(range(pix - 1, -1, -1))
    filtered, own, arrived = [None] * pix, None, []
    probe_half = probes.astype(BF16)
    images = pltpu.with_memory_space_constraint(images, pltpu.HBM)
    for shift in shifts:
        filtered[shift], part = filter_and_score(
            places,
            rows_at + shift,
            images,
            classes,
            ctf_table,
            probe_half,
            chunk,
            BF16 if shift else F32,
        )
        if shift:
            arrived.append(row_halves(xor_swap(part, "pix", shift)))
        else:
            own = row_halves(part)

    basis = inverse = None
    for sweep in range(ITERS):
        share = []
        for at in (0, 1):
            total = own[at]
            for part in arrived:
                total = total + part[at].astype(F32)
            here = weight_share[at] if sweep == 0 else weight_share[at] * RANGE
            share.append((here * total).astype(BF16))
        scaled = spread(share, pix)

        rows_of = [(at, half) for at in range(pix) for half in (0, 1)]
        early_rows = [(1, 0), (2, 1)] if pix == 4 else rows_of[2:pix]
        late_rows = [row for row in rows_of[2:] if row not in early_rows]
        early = early_sum(places, pairs_at, filtered, scaled, rows_of[:2], width, [])
        if early_rows:
            early = early_sum(
                places, pairs_at, filtered, scaled, early_rows, width, [early]
            )
        parts, relay, after = [], None, []
        for s in level_order(depth):
            send, keep = late_sum(
                places,
                pairs_at + 2 * s,
                2 * s,
                filtered,
                scaled,
                late_rows,
                early,
                width,
                after[-2:-1],
            )
            both = keep + xor_swap(send, "img", 1).astype(F32)
            after.append(both)
            if s == 0:
                parts.append(row_halves(both))
            elif depth == 4 and s == 3:
                relay = send_sum(both, s, depth, None)
            else:
                parts.append(send_sum(both, s, depth, relay))

        if sweep == ITERS - 1:
            gram = half_gram(places, cores_at, basis)
            gram = add_over_pix(gram, pix)
            other = xor_swap(gram, "img", 1)
            _, inverse = cholesky_and_inverse(places, cores_at, [gram, other], 1)
            break

        total = [sum(part[at].astype(F32) for part in parts) for at in (0, 1)]
        block = jnp.concatenate(total, 0).astype(BF16)
        basis = gather_cores(gather_levels(block, depth), depth)

        own, arrived = score_and_scatter(places, gathered_at, filtered, basis, pix)

    half, send, keep = normalize_and_gram(places, cores_at, sum(parts, []), inverse, 1.0 / RANGE)
    gram = keep + xor_swap(send, "img", 1)
    step = 1
    while step < depth:
        gram = gram + xor_swap(gram, "img", 2 * step)
        step *= 2
    gram = add_over_pix(gram, pix)
    other = xor_swap(gram, "img", 1)
    near = [half] + [xor_swap(half, "img", 2 * s) for s in range(1, depth)]
    basis = near + [xor_swap(block, "img", 1) for block in near]
    factor, inverse = cholesky_and_inverse(places, cores_at, [gram, other], 1)
    return apply_inverse(places, gathered_at, inverse, basis), factor


def plain_per_device(images, classes, ctf_table, weights, probes):
    onehot = (classes[:, None] == jnp.arange(ctf_table.shape[0])[None, :]).astype(BF16)
    filters = jnp.dot(onehot, ctf_table, preferred_element_type=F32)
    filtered = (images.astype(F32) * filters).astype(BF16)
    current = probes
    factor = None
    for _ in range(ITERS):
        share_rows = filtered.shape[0] // lax.axis_size("pix")
        shares = lax.psum_scatter(
            jnp.dot(filtered, current.astype(BF16), preferred_element_type=F32),
            "pix",
            scatter_dimension=0,
            tiled=True,
        )
        weight_share = lax.dynamic_slice_in_dim(
            weights, lax.axis_index("pix") * share_rows, share_rows, 0
        )
        scaled_share = (weight_share[:, None] * shares).astype(BF16)
        scaled = lax.all_gather(scaled_share, "pix", axis=0, tiled=True)
        image_sum = lax.psum(contract_rows(filtered, scaled), "img")
        gram = lax.psum(jnp.dot(image_sum.T, image_sum, precision=HIGHEST), "pix")
        factor = jnp.linalg.cholesky(gram)
        current = jax.scipy.linalg.solve_triangular(factor, image_sum.T, lower=True).T
    return current, factor


def power_of_two(n):
    return n > 1 and n & (n - 1) == 0


def fits(rows, pixels, columns, pix, img):
    return (
        power_of_two(pix)
        and power_of_two(img)
        and rows % (32 * pix) == 0
        and pixels % (LANES * img) == 0
        and columns % LANES == 0
        and columns % (8 * img) == 0
    )


def per_device_of(images, classes, ctf_table, weights, probes):
    pix, img = lax.axis_size("pix"), lax.axis_size("img")
    if not fits(*images.shape, probes.shape[1], pix, img):
        return plain_per_device(images, classes, ctf_table, weights, probes)
    return per_device(images, classes, ctf_table, weights, probes)


def solution(mesh):
    in_specs = (P("img", "pix"), P("img"), P(None, "pix"), P("img"), P("pix", None))
    out_specs = (P("pix", None), P())
    return jax.shard_map(
        per_device_of, mesh=mesh, in_specs=in_specs, out_specs=out_specs, check_vma=False
    )
```
